32 devices in a mesh: pop: 16 (over z, y, core), tp: 2 (over x).
Axes of the slice: x: 2, y: 2, z: 4, core: 2. Of those that a mesh axis runs over, the one named last changes fastest.
Arguments:
- tokens: bfloat16 [16, 512, 1792], P('pop', None, 'tp'), may hold values from -6 to 6
- weight: bfloat16 [16, 1792, 7168], P('pop', 'tp'), may hold values from -0.125 to 0.125
- momentum: bfloat16 [16, 1792, 7168], P('pop', 'tp'), may hold values from -6 to 6
- cotangent: bfloat16 [16, 512, 7168], P('pop', None, 'tp'), may hold values from -0.5 to 0.5
- assignment: int32 [4, 2], replicated, may hold values from 0 to 15, as said below
- lr_index: int32 [16], replicated, may hold values from 0 to 7
- rates: float32 [8], replicated, may hold values from 0.01 to 0.1
Outputs:
- activation: bfloat16 [16, 512, 7168], P('pop', None, 'tp')
- new_weight: bfloat16 [16, 1792, 7168], P('pop', 'tp')
The draws below stay inside these ranges and needn't reach their ends.
Inputs may be any that keep to these rules, and one draw needn't show every extreme that they name: `assignment`: column 0 names 4 distinct members; column 1 names exactly 1 distinct members, each in some row, none of them in column 0.
All inputs are finite; a program needn't handle non-finite values.
Results may differ from the reference program's by a relative error of at most 0.015.
Values may be sent and summed in bfloat16 or wider, within the bound.
A program may use at most 192 MiB of HBM per device.

```python
import math
import jax
import jax.numpy as jnp
from jax import lax

D = 1792
FF = 7168
TOK = 512
RATES = 8
MEMBERS = 16
LOSERS = 4
TOPS = 1
N_TP = 2


def draw_assignment(key, part):
    chosen_count = TOPS + LOSERS
    middle = jax.random.permutation(jax.random.fold_in(key, 11), MEMBERS - 2).astype(jnp.int32) + 1
    ends = jnp.array([0, MEMBERS - 1], dtype=jnp.int32)
    picked = jnp.concatenate([ends, middle[:chosen_count - 2]]).astype(jnp.int32)
    shuffle = jax.random.permutation(jax.random.fold_in(key, 13), chosen_count).astype(jnp.int32)
    order = picked[shuffle]
    winners_set = order[:TOPS]
    losers = order[TOPS:TOPS + LOSERS]
    picks = jax.random.randint(jax.random.fold_in(key, 12), (LOSERS,), 0, TOPS)
    rows = jnp.arange(LOSERS, dtype=jnp.int32)
    picks = jnp.where(rows < TOPS, rows, picks).astype(jnp.int32)
    winners = winners_set[picks]
    return jnp.stack([losers, winners], axis=1).astype(jnp.int32)


def plant(values, rng, low, largest):
    extent = values.shape
    place = [jax.random.randint(jax.random.fold_in(rng, axis), (), 0, extent[axis]) for axis in range(len(extent))]
    values = values.at[tuple(place)].set(low)
    longest = extent.index(max(extent))
    place[longest] = (place[longest] + 1) % extent[longest]
    return values.at[tuple(place)].set(largest)


def block_levels(rng, shape, pieces, least, high):
    loudness, own = 1.0, jax.random.fold_in(rng, 6)
    for axis_at, blocks in pieces:
        steps = jnp.exp(jax.random.uniform(jax.random.fold_in(own, axis_at), (blocks,), jnp.float32, least / len(pieces), high / len(pieces)))
        loudness = loudness * jnp.repeat(steps, shape[axis_at] // blocks).reshape([-1 if axis == axis_at else 1 for axis in range(len(shape))])
    return loudness


def centred(rng, dims, width, limit, shards=(), kind=jnp.bfloat16):
    drawn = width * jax.random.normal(rng, dims, jnp.float32)
    if shards:
        drawn = drawn * block_levels(rng, dims, shards, -0.22, 0.18)
    return jnp.clip(drawn, -limit, limit).astype(kind)


def setup_inputs(seed: int = 0) -> dict:
    arg_keys = jax.random.split(jax.random.key(seed), 8)
    return {
        "tokens": centred(arg_keys[0], (MEMBERS, TOK, D), 1.0, 6.0, ((0, 16), (2, 2))),
        "weight": centred(arg_keys[1], (MEMBERS, D, FF), D ** -0.5, 0.125, ((0, 16), (1, 2))),
        "momentum": centred(arg_keys[2], (MEMBERS, D, FF), 1.0, 6.0, ((0, 16), (1, 2))),
        "cotangent": centred(arg_keys[3], (MEMBERS, TOK, FF), 0.0625, 0.5, ((0, 16), (2, 2))),
        "assignment": draw_assignment(jax.random.fold_in(arg_keys[7], 71), 0),
        "lr_index": plant(jax.random.randint(arg_keys[5], (MEMBERS,), 0, RATES), jax.random.fold_in(arg_keys[5], 1), 0, RATES - 1).astype(jnp.int32),
        "rates": jnp.clip(jnp.exp(jax.random.uniform(arg_keys[6], (RATES,), jnp.float32, math.log(0.01), math.log(0.1))), 0.01, 0.1),
    }


def gelu_tanh(value):
    return jax.nn.gelu(value, approximate=True)

def reference(tokens, weight, momentum, cotangent, assignment, lr_index, rates):
    member_ids = jnp.arange(MEMBERS, dtype=jnp.int32)
    hit = assignment[:, 0][None, :] == member_ids[:, None]
    source_all = jnp.where(jnp.any(hit, axis=1), lax.optimization_barrier(jnp.sum(jnp.where(hit, assignment[:, 1][None, :], 0), axis=1)).astype(jnp.int32), member_ids)
    rate_ids = jnp.arange(RATES, dtype=jnp.int32)
    rate_all = lax.optimization_barrier(jnp.sum(jnp.where(rate_ids[None, :] == lr_index[:, None], rates[None, :], 0.0), axis=1))
    block = D // N_TP

    def one_member(member):
        source = source_all[member]
        inputs = tokens[member]
        taken_weight = weight[source]
        taken_momentum = momentum[source]
        hidden = jnp.zeros((TOK, FF), jnp.float32)
        for piece in range(N_TP):
            partial_value = jnp.dot(inputs[:, piece * block:(piece + 1) * block], taken_weight[piece * block:(piece + 1) * block], preferred_element_type=jnp.float32).astype(jnp.bfloat16)
            hidden = hidden + lax.optimization_barrier(partial_value).astype(jnp.float32)
        active, pullback = jax.vjp(gelu_tanh, hidden)
        grad_hidden = pullback(cotangent[member].astype(jnp.float32))[0].astype(jnp.bfloat16)
        grad_weight = jnp.dot(inputs.T, grad_hidden, preferred_element_type=jnp.float32)
        new_momentum = 0.9 * taken_momentum.astype(jnp.float32) + grad_weight
        updated = (taken_weight.astype(jnp.float32) - rate_all[member] * new_momentum).astype(jnp.bfloat16)
        return (active.astype(jnp.bfloat16), updated)
    activation, new_weight = lax.map(one_member, member_ids)
    return (activation, new_weight)
```

```python
import functools
import math

import jax
import jax.numpy as jnp
from jax import lax
from jax.experimental import pallas as pl
from jax.experimental.pallas import tpu as pltpu
from jax.sharding import PartitionSpec as P

MESH = pl.DeviceIdType.MESH
PIECES = 4
TILE = 512


def ring_of(member, members):
    core = member % 2
    y = (member // 2) % 2
    z = member // 4
    half = members // 4
    chip = z * (1 - y) + (2 * half - 1 - z) * y
    return 2 * chip + core


def member_at(place, members):
    core = place % 2
    chip = place // 2
    half = members // 4
    y = chip // half
    z = chip * (1 - y) + (2 * half - 1 - chip) * y
    return (2 * z + y) * 2 + core


def gelu_tanh(value):
    return jax.nn.gelu(value, approximate=True)


def activate(hidden, cot_block):
    active, pullback = jax.vjp(gelu_tanh, hidden)
    grad_hidden = pullback(cot_block.astype(jnp.float32))[0].astype(jnp.bfloat16)
    return (active.astype(jnp.bfloat16), grad_hidden)


def rows_of(rows, cols, whole_cols):
    wanted = 16 * (whole_cols // cols)
    return wanted if (rows // 2) % wanted == 0 else 16


def spread_kernel(
    members, height, table, own, out, came, mirror, other, sent,
    send_sem, recv_sem, near_send, near_recv, back_send, back_recv,
):
    rows, cols = own.shape
    half = rows // 2
    blocks = half // height
    chips = members // 2
    steps = blocks + chips - 1
    width = cols // PIECES
    place = ring_of(lax.axis_index("pop"), members)
    chip = place // 2
    core = place % 2
    target = member_at(2 * ((chip + 1 - 2 * core + chips) % chips) + core, members)
    origin = member_at(2 * ((chip - 1 + 2 * core + chips) % chips) + core, members)
    partner = member_at(2 * chip + 1 - core, members)
    is_root = table[0] > 0
    chosen = table[1] > 0
    partner_root = table[4] > 0

    barrier = pltpu.get_barrier_semaphore()
    for near in (target, origin, partner):
        pl.semaphore_signal(barrier, inc=1, device_id={"pop": near}, device_id_type=MESH)
    pl.semaphore_wait(barrier, 3)

    def block_rows(way, block):
        return pl.ds(pl.multiple_of(way * half + block * height, height), height)

    def lend(block):
        return pltpu.make_async_remote_copy(
            src_ref=own.at[block_rows(1 - core, block), :],
            dst_ref=other.at[block],
            send_sem=near_send.at[block],
            recv_sem=near_recv.at[block],
            device_id={"pop": partner},
            device_id_type=MESH,
        )

    def onward(step, piece):
        cut = pl.ds(piece * width, width)
        return pltpu.make_async_remote_copy(
            src_ref=sent.at[step % 2, :, cut],
            dst_ref=came.at[step, :, cut],
            send_sem=send_sem.at[step % 2, piece],
            recv_sem=recv_sem.at[step, piece],
            device_id={"pop": target},
            device_id_type=MESH,
        )

    def across(step):
        return pltpu.make_async_remote_copy(
            src_ref=came.at[step],
            dst_ref=mirror.at[step],
            send_sem=back_send.at[step],
            recv_sem=back_recv.at[step],
            device_id={"pop": partner},
            device_id_type=MESH,
        )

    def each(count, act):
        def body(index, carry):
            act(index)
            return carry

        lax.fori_loop(0, count, body, 0)

    each(blocks, lambda block: lend(block).start())
    lend(0).wait_recv()
    for piece in range(PIECES):
        cut = pl.ds(piece * width, width)
        sent[0, :, cut] = jnp.where(is_root, own[block_rows(core, 0), cut], other[0, :, cut])
        onward(0, piece).start()

    def forward(step, carry):
        block = jnp.minimum(step, blocks - 1)

        @pl.when(step < blocks)
        def _():
            lend(step).wait_recv()

        for piece in range(PIECES):
            cut = pl.ds(piece * width, width)
            onward(step - 1, piece).wait_recv()

            @pl.when(step >= 2)
            def _():
                onward(step - 2, piece).wait_send()

            relayed = jnp.where(partner_root, other[block, :, cut], came[step - 1, :, cut])
            sent[step % 2, :, cut] = jnp.where(
                is_root, own[block_rows(core, block), cut], relayed
            )
            onward(step, piece).start()
        across(step - 1).start()
        return carry

    lax.fori_loop(1, steps, forward, 0)
    for piece in range(PIECES):
        onward(steps - 1, piece).wait_recv()
    across(steps - 1).start()

    def settle(block):
        at = block_rows(core, block)
        out[at, :] = jnp.where(chosen, came[block + table[2 + core]], own[at, :])

    each(blocks, settle)
    each(steps, lambda step: across(step).wait_recv())

    def settle_other(block):
        at = block_rows(1 - core, block)
        out[at, :] = jnp.where(chosen, mirror[block + table[3 - core]], own[at, :])

    each(blocks, settle_other)
    for piece in range(PIECES):
        onward(steps - 2, piece).wait_send()
        onward(steps - 1, piece).wait_send()
    each(blocks, lambda block: lend(block).wait_send())
    each(steps, lambda step: across(step).wait_send())


def spread(value, table, members, turn, part, parts):
    rows, whole_cols = value.shape
    cols = whole_cols // parts
    height = rows_of(rows, cols, whole_cols)
    blocks = rows // 2 // height
    steps = blocks + members // 2 - 1
    return pl.pallas_call(
        functools.partial(spread_kernel, members, height),
        grid=(1,),
        out_shape=jax.ShapeDtypeStruct((rows, cols), value.dtype),
        in_specs=[
            pl.BlockSpec(memory_space=pltpu.SMEM),
            pl.BlockSpec((rows, cols), lambda i: (0, part), pipeline_mode=pl.Buffered(1)),
        ],
        out_specs=pl.BlockSpec((rows, cols), lambda i: (0, 0), pipeline_mode=pl.Buffered(1)),
        scratch_shapes=[
            pltpu.VMEM((steps, height, cols), value.dtype),
            pltpu.VMEM((steps, height, cols), value.dtype),
            pltpu.VMEM((blocks, height, cols), value.dtype),
            pltpu.VMEM((2, height, cols), value.dtype),
            pltpu.SemaphoreType.DMA((2, PIECES)),
            pltpu.SemaphoreType.DMA((steps, PIECES)),
            pltpu.SemaphoreType.DMA((blocks,)),
            pltpu.SemaphoreType.DMA((blocks,)),
            pltpu.SemaphoreType.DMA((steps,)),
            pltpu.SemaphoreType.DMA((steps,)),
        ],
        compiler_params=pltpu.CompilerParams(
            collective_id=turn, has_side_effects=True, vmem_limit_bytes=60 * 2**20
        ),
        cost_estimate=pl.CostEstimate(
            flops=0, bytes_accessed=300 * 2**20 // parts, transcendentals=0
        ),
        name=f"spread_{turn}",
    )(table, value)


def update_kernel(half, side, rate, turned, mine, theirs, weight, first, second, out):
    block = pl.program_id(0)
    grad = jnp.where(block // half == side[0], mine[...], theirs[...])
    grad_weight = jnp.dot(turned[...], grad, preferred_element_type=jnp.float32)
    momentum = jnp.where(block < half, first[...], second[...]).astype(jnp.float32)
    new_momentum = 0.9 * momentum + grad_weight
    out[...] = (weight[...].astype(jnp.float32) - rate[0] * new_momentum).astype(out.dtype)


def update(side, rate, turned, mine, theirs, weight, first, second):
    rows, cols = weight.shape
    tokens = turned.shape[1]
    half = cols // 2 // TILE
    near = lambda j, side: (0, jnp.clip(j - side[0] * half, 0, half - 1))
    far = lambda j, side: (0, jnp.clip(j - (1 - side[0]) * half, 0, half - 1))
    return pl.pallas_call(
        functools.partial(update_kernel, half),
        grid_spec=pltpu.PrefetchScalarGridSpec(
            num_scalar_prefetch=1,
            grid=(2 * half,),
            in_specs=[
                pl.BlockSpec(memory_space=pltpu.SMEM),
                pl.BlockSpec((rows, tokens), lambda j, side: (0, 0)),
                pl.BlockSpec((tokens, TILE), near),
                pl.BlockSpec((tokens, TILE), far),
                pl.BlockSpec((rows, TILE), lambda j, side: (0, j)),
                pl.BlockSpec((rows, TILE), lambda j, side: (0, jnp.minimum(j, half - 1))),
                pl.BlockSpec((rows, TILE), lambda j, side: (0, jnp.maximum(j - half, 0))),
            ],
            out_specs=pl.BlockSpec((rows, TILE), lambda j, side: (0, j)),
        ),
        out_shape=jax.ShapeDtypeStruct(weight.shape, weight.dtype),
        compiler_params=pltpu.CompilerParams(vmem_limit_bytes=40 * 2**20),
        cost_estimate=pl.CostEstimate(
            flops=2 * rows * cols * tokens,
            bytes_accessed=6 * rows * cols,
            transcendentals=0,
        ),
        name="update",
    )(side, rate, turned, mine, theirs, weight, first, second)


SUB = 128
CHUNK = 256
SPLIT = 2
DEPTH = 4
LAG = 4
LENT = 4
THROTTLE = 8
GRAD_FIRST = 34
GRAD_EVERY = 2


def fused_kernel(
    members, assign, tokens, weight, momentum, cot,
    both, grads, act, turned,
    hold, mirror, own, other, taken, theirs, came, mine, cot_v, tok_v, turn_v,
    own_sem, lend_send, lend_recv, ring_send, ring_recv, back_send, back_recv,
    x_send, x_recv, g_send, g_recv, out_sem, act_sem, grad_sem, load_sem,
):
    rows, cols = weight.shape
    half = rows // 2
    part = half // SPLIT
    chunks = cols // CHUNK
    own_chunks = chunks // 2
    per = SPLIT * (CHUNK // SUB)
    all_chunks = 2 * chunks
    units = all_chunks * per
    chips = members // 2
    fill = (chips - 1) * DEPTH
    steps = units + fill
    behind = (fill + LAG) // per
    slots = own.shape[0]

    me = lax.axis_index("pop")
    side = lax.axis_index("tp")
    place = ring_of(me, members)
    chip = place // 2
    core = place % 2
    target = member_at(2 * ((chip + 1 - 2 * core + chips) % chips) + core, members)
    origin = member_at(2 * ((chip - 1 + 2 * core + chips) % chips) + core, members)
    partner = member_at(2 * chip + 1 - core, members)

    root = assign[0, 1]
    root_chip = ring_of(root, members) // 2
    is_root = me == root
    partner_root = partner == root
    chosen = assign[0, 0] == me
    for row in range(1, assign.shape[0]):
        chosen = jnp.logical_or(chosen, assign[row, 0] == me)
    forward_gap = (chip - root_chip + chips) % chips
    backward_gap = (root_chip - chip + chips) % chips
    own_gap = jnp.where(core == 0, forward_gap, backward_gap)
    mirror_gap = jnp.where(core == 0, backward_gap, forward_gap)

    def column(chunk):
        at = chunk % chunks
        first = at < own_chunks
        return jnp.where(first, (1 - side) * own_chunks + at, side * own_chunks + at - own_chunks)

    def half_rows(way, piece):
        return pl.ds(pl.multiple_of(way * half + piece * part, 16), part)

    def load_own(source, chunk):
        cut = pl.ds(pl.multiple_of(column(chunk) * CHUNK, CHUNK), CHUNK)
        slot = chunk % slots
        return pltpu.make_async_copy(source.at[:, cut], own.at[slot], own_sem.at[slot])

    def start_own(chunk):
        @pl.when(chunk < chunks)
        def _():
            load_own(weight, chunk).start()

        @pl.when(chunk >= chunks)
        def _():
            load_own(momentum, chunk).start()

    def lend(chunk):
        away = pl.ds(pl.multiple_of((1 - core) * half, 16), half)
        return pltpu.make_async_remote_copy(
            src_ref=own.at[chunk % slots, away, :],
            dst_ref=other.at[chunk % LENT],
            send_sem=lend_send.at[chunk % LENT],
            recv_sem=lend_recv.at[chunk],
            device_id={"pop": partner},
            device_id_type=MESH,
        )

    def onward(step):
        return pltpu.make_async_remote_copy(
            src_ref=hold.at[step],
            dst_ref=hold.at[step + DEPTH],
            send_sem=ring_send.at[step % THROTTLE],
            recv_sem=ring_recv.at[step + DEPTH],
            device_id={"pop": target},
            device_id_type=MESH,
        )

    def across(step):
        return pltpu.make_async_remote_copy(
            src_ref=hold.at[step],
            dst_ref=mirror.at[step],
            send_sem=back_send.at[step % THROTTLE],
            recv_sem=back_recv.at[step],
            device_id={"pop": partner},
            device_id_type=MESH,
        )

    def trade(piece):
        return pltpu.make_async_remote_copy(
            src_ref=theirs.at[piece],
            dst_ref=came.at[piece],
            send_sem=x_send.at[piece],
            recv_sem=x_recv.at[piece],
            device_id={"tp": 1 - side},
            device_id_type=MESH,
        )

    def trade_grad(piece):
        at = side * own_chunks + piece
        return pltpu.make_async_remote_copy(
            src_ref=mine.at[piece],
            dst_ref=grads.at[at],
            send_sem=g_send.at[piece],
            recv_sem=g_recv.at[piece],
            device_id={"tp": 1 - side},
            device_id_type=MESH,
        )

    def arrived_grad(piece):
        at = (1 - side) * own_chunks + piece
        return pltpu.make_async_remote_copy(
            src_ref=mine.at[piece],
            dst_ref=grads.at[at],
            send_sem=g_send.at[piece],
            recv_sem=g_recv.at[piece],
            device_id={"tp": 1 - side},
            device_id_type=MESH,
        )

    def keep_grad(piece):
        return pltpu.make_async_copy(
            mine.at[piece], grads.at[side * own_chunks + piece], grad_sem.at[piece]
        )

    def keep_act(piece):
        return pltpu.make_async_copy(came.at[piece], act.at[piece], act_sem.at[piece])

    def keep_taken(chunk):
        place_at = column(chunk) + chunks * (chunk // chunks)
        return pltpu.make_async_copy(
            taken.at[chunk % 3], both.at[place_at], out_sem.at[chunk % 3]
        )

    load_tokens = pltpu.make_async_copy(tokens, tok_v, load_sem.at[0])
    load_cot = pltpu.make_async_copy(cot, cot_v, load_sem.at[1])
    keep_turned = pltpu.make_async_copy(turn_v, turned, load_sem.at[2])

    load_own(weight, 0).start()
    load_tokens.start()
    load_own(weight, 1).start()
    load_own(weight, 2).start()
    load_cot.start()
    barrier = pltpu.get_barrier_semaphore()
    for near in (target, origin, partner):
        pl.semaphore_signal(barrier, inc=1, device_id={"pop": near}, device_id_type=MESH)
    pl.semaphore_signal(barrier, inc=1, device_id={"tp": 1 - side}, device_id_type=MESH)
    pl.semaphore_wait(barrier, 4)
    load_own(weight, 0).wait()
    lend(0).start()
    load_tokens.wait()

    def ring_step(chunk, sub, step):
        piece = sub % SPLIT
        cut = pl.ds((sub // SPLIT) * SUB, SUB)

        @pl.when(jnp.logical_and(step >= DEPTH, step < steps))
        def _():
            onward(step - DEPTH).wait_recv()

        @pl.when(jnp.logical_and(chunk < all_chunks, step < DEPTH))
        def _():
            held = own[chunk % slots, half_rows(core, piece), cut]
            lent = other[chunk % LENT, pl.ds(piece * part, part), cut]
            hold[step] = jnp.where(is_root, held, lent)

        @pl.when(jnp.logical_and(chunk < all_chunks, step >= DEPTH))
        def _():
            held = own[chunk % slots, half_rows(core, piece), cut]
            lent = other[chunk % LENT, pl.ds(piece * part, part), cut]
            hold[step] = jnp.where(is_root, held, jnp.where(partner_root, lent, hold[step]))

        @pl.when(step + DEPTH < steps)
        def _():
            @pl.when(step >= THROTTLE)
            def _():
                onward(step - THROTTLE).wait_send()

            onward(step).start()

        @pl.when(step < steps)
        def _():
            @pl.when(step >= THROTTLE)
            def _():
                across(step - THROTTLE).wait_send()

            across(step).start()

        @pl.when(jnp.logical_and(step >= LAG, step < steps + LAG))
        def _():
            across(step - LAG).wait_recv()

    def consume(chunk, sub):
        piece = sub % SPLIT
        cut = pl.ds((sub // SPLIT) * SUB, SUB)
        unit = chunk * per + sub
        for way, source, gap in ((core, hold, own_gap), (1 - core, mirror, mirror_gap)):
            value = source[unit]
            for hop in range(1, chips):
                value = jnp.where(gap == hop, source[unit + hop * DEPTH], value)
            held = own[chunk % slots, half_rows(way, piece), cut]
            taken[chunk % 3, half_rows(way, piece), cut] = jnp.where(chosen, value, held)

    def finish(chunk):
        @pl.when(chunk < chunks)
        def _():
            value = jnp.dot(
                tok_v[...], taken[chunk % 3], preferred_element_type=jnp.float32
            ).astype(jnp.bfloat16)

            @pl.when(chunk < own_chunks)
            def _():
                theirs[chunk] = value
                trade(chunk).start()

            @pl.when(chunk >= own_chunks)
            def _():
                mine[chunk - own_chunks] = value

        keep_taken(chunk).start()

    def gradient(piece):
        trade(piece).wait_recv()
        cut = pl.ds(pl.multiple_of(piece * CHUNK, CHUNK), CHUNK)
        tall = 64

        def strip(index, carry):
            at = pl.ds(pl.multiple_of(index * tall, tall), tall)
            value = mine[piece, at, :].astype(jnp.float32) + came[piece, at, :].astype(jnp.float32)
            slope = math.sqrt(2 / math.pi)
            square = value * value
            bent = jnp.tanh(slope * (value + 0.044715 * (square * value)))
            gate = 0.5 * (1.0 + bent)
            rise = 0.5 * value * (1.0 - bent * bent) * (slope * (1.0 + 0.134145 * square))
            came[piece, at, :] = (value * gate).astype(jnp.bfloat16)
            mine[piece, at, :] = (cot_v[at, cut].astype(jnp.float32) * (gate + rise)).astype(
                jnp.bfloat16
            )
            return carry

        lax.fori_loop(0, tok_v.shape[0] // tall, strip, 0)
        trade_grad(piece).start()
        keep_grad(piece).start()
        keep_act(piece).start()

    def turn(chunk, carry):
        @pl.when(chunk < all_chunks)
        def _():
            @pl.when(chunk >= LENT - 1)
            def _():
                lend(chunk - LENT + 1).wait_send()

            @pl.when(chunk + 1 < all_chunks)
            def _():
                load_own(weight, chunk + 1).wait()
                lend(chunk + 1).start()

            @pl.when(chunk + 3 < all_chunks)
            def _():
                start_own(chunk + 3)

            lend(chunk).wait_recv()

        late = chunk - behind

        @pl.when(late >= 3)
        def _():
            keep_taken(late - 3).wait()

        for sub in range(per):
            ring_step(chunk, sub, chunk * per + sub)

            @pl.when(late >= 0)
            def _():
                consume(late, sub)

        @pl.when(late >= 0)
        def _():
            finish(late)

        @pl.when(chunk == 2)
        def _():
            turn_v[...] = tok_v[...].T
            keep_turned.start()

        @pl.when(chunk == GRAD_FIRST - 1)
        def _():
            load_cot.wait()

        since = chunk - GRAD_FIRST

        @pl.when(
            jnp.logical_and(
                since >= 0,
                jnp.logical_and(since % GRAD_EVERY == 0, since // GRAD_EVERY < own_chunks),
            )
        )
        def _():
            gradient(since // GRAD_EVERY)

        return carry

    lax.fori_loop(0, all_chunks + behind, turn, 0)

    for step in range(steps - DEPTH - THROTTLE, steps - DEPTH):
        onward(step).wait_send()
    for step in range(steps - THROTTLE, steps):
        across(step).wait_send()
    for chunk in range(all_chunks - LENT + 1, all_chunks):
        lend(chunk).wait_send()
    for chunk in range(all_chunks - 3, all_chunks):
        keep_taken(chunk).wait()
    keep_turned.wait()

    def drain(piece, carry):
        trade(piece).wait_send()
        keep_act(piece).wait()
        keep_grad(piece).wait()
        trade_grad(piece).wait_send()
        arrived_grad(piece).wait_recv()
        return carry

    lax.fori_loop(0, own_chunks, drain, 0)


def fused(assignment, tokens, weight, momentum, cot, members):
    rows, cols = weight.shape
    count, share = cot.shape
    chunks = cols // CHUNK
    own_chunks = chunks // 2
    per = SPLIT * (CHUNK // SUB)
    chips = members // 2
    fill = (chips - 1) * DEPTH
    steps = 2 * chunks * per + fill
    slots = (fill + LAG) // per + 4
    part = rows // 2 // SPLIT
    kind = weight.dtype
    dma = pltpu.SemaphoreType.DMA
    anywhere = pl.BlockSpec(memory_space=pl.ANY)
    return pl.pallas_call(
        functools.partial(fused_kernel, members),
        out_shape=(
            jax.ShapeDtypeStruct((2 * chunks, rows, CHUNK), kind),
            jax.ShapeDtypeStruct((chunks, count, CHUNK), kind),
            jax.ShapeDtypeStruct((own_chunks, count, CHUNK), kind),
            jax.ShapeDtypeStruct((rows, count), kind),
        ),
        in_specs=[pl.BlockSpec(memory_space=pltpu.SMEM)] + [anywhere] * 4,
        out_specs=(anywhere,) * 4,
        scratch_shapes=[
            pltpu.VMEM((steps, part, SUB), kind),
            pltpu.VMEM((steps, part, SUB), kind),
            pltpu.VMEM((slots, rows, CHUNK), kind),
            pltpu.VMEM((LENT, rows // 2, CHUNK), kind),
            pltpu.VMEM((3, rows, CHUNK), kind),
            pltpu.VMEM((own_chunks, count, CHUNK), kind),
            pltpu.VMEM((own_chunks, count, CHUNK), kind),
            pltpu.VMEM((own_chunks, count, CHUNK), kind),
            pltpu.VMEM((count, share), kind),
            pltpu.VMEM((count, rows), kind),
            pltpu.VMEM((rows, count), kind),
            dma((slots,)),
            dma((LENT,)),
            dma((2 * chunks,)),
            dma((THROTTLE,)),
            dma((steps,)),
            dma((THROTTLE,)),
            dma((steps,)),
            dma((own_chunks,)),
            dma((own_chunks,)),
            dma((own_chunks,)),
            dma((own_chunks,)),
            dma((3,)),
            dma((own_chunks,)),
            dma((own_chunks,)),
            dma((3,)),
        ],
        compiler_params=pltpu.CompilerParams(
            collective_id=0, has_side_effects=True, vmem_limit_bytes=60 * 2**20
        ),
        name="fused",
    )(assignment, tokens, weight, momentum, cot)


def settle_kernel(lr_index, rates, turned, weight, momentum, grads, act, out, active):
    rate = rates[lr_index[lax.axis_index("pop")]]
    for piece in range(weight.shape[0]):
        cut = pl.ds(piece * CHUNK, CHUNK)
        grad_weight = jnp.dot(turned[...], grads[piece], preferred_element_type=jnp.float32)
        new_momentum = 0.9 * momentum[piece].astype(jnp.float32) + grad_weight
        out[:, cut] = (weight[piece].astype(jnp.float32) - rate * new_momentum).astype(out.dtype)
    active[...] = act[0]


def settle(lr_index, rates, turned, both, grads, act):
    rows, count = turned.shape
    chunks = both.shape[0] // 2
    own_chunks = act.shape[0]
    group = chunks // own_chunks
    wide = group * CHUNK
    scalar = pl.BlockSpec(memory_space=pltpu.SMEM)
    return pl.pallas_call(
        settle_kernel,
        grid=(own_chunks,),
        in_specs=[
            scalar,
            scalar,
            pl.BlockSpec((rows, count), lambda j: (0, 0)),
            pl.BlockSpec((group, rows, CHUNK), lambda j: (j, 0, 0)),
            pl.BlockSpec((group, rows, CHUNK), lambda j: (j + own_chunks, 0, 0)),
            pl.BlockSpec((group, count, CHUNK), lambda j: (j, 0, 0)),
            pl.BlockSpec((1, count, CHUNK), lambda j: (j, 0, 0)),
        ],
        out_specs=(
            pl.BlockSpec((rows, wide), lambda j: (0, j)),
            pl.BlockSpec((count, CHUNK), lambda j: (0, j)),
        ),
        out_shape=(
            jax.ShapeDtypeStruct((rows, chunks * CHUNK), both.dtype),
            jax.ShapeDtypeStruct((count, own_chunks * CHUNK), both.dtype),
        ),
        compiler_params=pltpu.CompilerParams(vmem_limit_bytes=40 * 2**20),
        name="settle",
    )(lr_index, rates, turned, both, both, grads, act)


def local(tokens, weight, momentum, cotangent, assignment, lr_index, rates):
    members = lax.axis_size("pop")
    ranks = lax.axis_size("tp")
    me = lax.axis_index("pop")
    side = lax.axis_index("tp")
    if ranks == 2 and assignment.shape[0] // 4 == 1:
        both, grads, act, turned = fused(
            assignment, tokens[0], weight[0], momentum[0], cotangent[0], members
        )
        updated, active = settle(lr_index, rates, turned, both, grads, act)
        return (active[None], updated[None])
    member_ids = jnp.arange(members, dtype=jnp.int32)
    hit = assignment[:, 0] == me
    my_source = jnp.where(jnp.any(hit), jnp.sum(jnp.where(hit, assignment[:, 1], 0)), me)
    my_index = jnp.sum(jnp.where(member_ids == me, lr_index, 0))
    rate_ids = jnp.arange(rates.shape[0], dtype=jnp.int32)
    my_rate = jnp.sum(jnp.where(rate_ids == my_index, rates, 0.0))
    tops = assignment.shape[0] // 4
    winner_hit = assignment[:, 1][None, :] == member_ids[:, None]
    present = jnp.any(winner_hit, axis=1)
    roots = jnp.sort(jnp.where(present, member_ids, members))[:tops]
    place = ring_of(me, members)
    tables = []
    for turn in range(tops):
        root = roots[turn]
        chips = members // 2
        root_place = ring_of(root, members)
        behind = (place // 2 - root_place // 2 + chips) % chips
        entries = (
            me == root,
            jnp.logical_and(my_source == root, me != root),
            (behind + chips - 1) % chips,
            (2 * chips - behind - 1) % chips,
            jnp.logical_and(place // 2 == root_place // 2, me != root),
        )
        tables.append(jnp.stack([entry.astype(jnp.int32) for entry in entries]))

    def take(value, first, part=0, parts=1):
        taken = None
        for turn in range(tops):
            arrived = spread(value, tables[turn], members, first + turn, part, parts)
            if taken is None:
                taken = arrived
            else:
                taken = jnp.where(my_source == roots[turn], arrived, taken)
        return taken

    inputs = tokens[0]
    share_cols = cotangent.shape[2]
    taken_weight = take(weight[0], 0)
    partial_value = jnp.dot(inputs, taken_weight, preferred_element_type=jnp.float32)
    partial_value = partial_value.astype(jnp.bfloat16)
    if ranks == 2:
        swap = [(0, 1), (1, 0)]
        left, right = partial_value[:, :share_cols], partial_value[:, share_cols:]
        mine = jnp.where(side == 0, left, right)
        theirs = jnp.where(side == 0, right, left)
        theirs, raw_momentum = lax.optimization_barrier((theirs, momentum[0]))
        arrived = lax.ppermute(theirs, "tp", swap)
        first = take(raw_momentum, tops, 0, 2)
        arrived, first = lax.optimization_barrier((arrived, first))
        hidden = mine.astype(jnp.float32) + arrived.astype(jnp.float32)
        active, grad_mine = activate(hidden, cotangent[0])
        grad_mine, raw_momentum = lax.optimization_barrier((grad_mine, raw_momentum))
        grad_theirs = lax.ppermute(grad_mine, "tp", swap)
        second = take(raw_momentum, 2 * tops, 1, 2)
        updated = update(
            side.astype(jnp.int32).reshape(1),
            my_rate.reshape(1),
            inputs.T,
            grad_mine,
            grad_theirs,
            taken_weight,
            first,
            second,
        )
    else:
        taken_momentum = take(momentum[0], tops)
        hidden = lax.psum_scatter(
            partial_value, "tp", scatter_dimension=1, tiled=True
        ).astype(jnp.float32)
        active, grad_mine = activate(hidden, cotangent[0])
        grad_hidden = lax.all_gather(grad_mine, "tp", axis=1, tiled=True)
        grad_weight = lax.dot_general(
            inputs, grad_hidden, (((0,), (0,)), ((), ())), preferred_element_type=jnp.float32
        )
        new_momentum = 0.9 * taken_momentum.astype(jnp.float32) + grad_weight
        updated = taken_weight.astype(jnp.float32) - my_rate * new_momentum
        updated = updated.astype(jnp.bfloat16)
    return (active[None], updated[None])


def solution(mesh):
    placed = (
        P("pop", None, "tp"),
        P("pop", "tp", None),
        P("pop", "tp", None),
        P("pop", None, "tp"),
        P(),
        P(),
        P(),
    )
    return jax.shard_map(
        local,
        mesh=mesh,
        in_specs=placed,
        out_specs=(P("pop", None, "tp"), P("pop", "tp", None)),
        check_vma=False,
    )
```

```python
import functools
import math

import jax
import jax.numpy as jnp
from jax import lax
from jax.experimental import pallas as pl
from jax.experimental.pallas import tpu as pltpu
from jax.sharding import PartitionSpec as P

MESH = pl.DeviceIdType.MESH
PIECES = 4
TILE = 512


def ring_of(member, members):
    core = member % 2
    y = (member // 2) % 2
    z = member // 4
    half = members // 4
    chip = z * (1 - y) + (2 * half - 1 - z) * y
    return 2 * chip + core


def member_at(place, members):
    core = place % 2
    chip = place // 2
    half = members // 4
    y = chip // half
    z = chip * (1 - y) + (2 * half - 1 - chip) * y
    return (2 * z + y) * 2 + core


def gelu_tanh(value):
    return jax.nn.gelu(value, approximate=True)


def activate(hidden, cot_block):
    active, pullback = jax.vjp(gelu_tanh, hidden)
    grad_hidden = pullback(cot_block.astype(jnp.float32))[0].astype(jnp.bfloat16)
    return (active.astype(jnp.bfloat16), grad_hidden)


def rows_of(rows, cols, whole_cols):
    wanted = 16 * (whole_cols // cols)
    return wanted if (rows // 2) % wanted == 0 else 16


def spread_kernel(
    members, height, table, own, out, came, mirror, other, sent,
    send_sem, recv_sem, near_send, near_recv, back_send, back_recv,
):
    rows, cols = own.shape
    half = rows // 2
    blocks = half // height
    chips = members // 2
    steps = blocks + chips - 1
    width = cols // PIECES
    place = ring_of(lax.axis_index("pop"), members)
    chip = place // 2
    core = place % 2
    target = member_at(2 * ((chip + 1 - 2 * core + chips) % chips) + core, members)
    origin = member_at(2 * ((chip - 1 + 2 * core + chips) % chips) + core, members)
    partner = member_at(2 * chip + 1 - core, members)
    is_root = table[0] > 0
    chosen = table[1] > 0
    partner_root = table[4] > 0

    barrier = pltpu.get_barrier_semaphore()
    for near in (target, origin, partner):
        pl.semaphore_signal(barrier, inc=1, device_id={"pop": near}, device_id_type=MESH)
    pl.semaphore_wait(barrier, 3)

    def block_rows(way, block):
        return pl.ds(pl.multiple_of(way * half + block * height, height), height)

    def lend(block):
        return pltpu.make_async_remote_copy(
            src_ref=own.at[block_rows(1 - core, block), :],
            dst_ref=other.at[block],
            send_sem=near_send.at[block],
            recv_sem=near_recv.at[block],
            device_id={"pop": partner},
            device_id_type=MESH,
        )

    def onward(step, piece):
        cut = pl.ds(piece * width, width)
        return pltpu.make_async_remote_copy(
            src_ref=sent.at[step % 2, :, cut],
            dst_ref=came.at[step, :, cut],
            send_sem=send_sem.at[step % 2, piece],
            recv_sem=recv_sem.at[step, piece],
            device_id={"pop": target},
            device_id_type=MESH,
        )

    def across(step):
        return pltpu.make_async_remote_copy(
            src_ref=came.at[step],
            dst_ref=mirror.at[step],
            send_sem=back_send.at[step],
            recv_sem=back_recv.at[step],
            device_id={"pop": partner},
            device_id_type=MESH,
        )

    def each(count, act):
        def body(index, carry):
            act(index)
            return carry

        lax.fori_loop(0, count, body, 0)

    each(blocks, lambda block: lend(block).start())
    lend(0).wait_recv()
    for piece in range(PIECES):
        cut = pl.ds(piece * width, width)
        sent[0, :, cut] = jnp.where(is_root, own[block_rows(core, 0), cut], other[0, :, cut])
        onward(0, piece).start()

    def forward(step, carry):
        block = jnp.minimum(step, blocks - 1)

        @pl.when(step < blocks)
        def _():
            lend(step).wait_recv()

        for piece in range(PIECES):
            cut = pl.ds(piece * width, width)
            onward(step - 1, piece).wait_recv()

            @pl.when(step >= 2)
            def _():
                onward(step - 2, piece).wait_send()

            relayed = jnp.where(partner_root, other[block, :, cut], came[step - 1, :, cut])
            sent[step % 2, :, cut] = jnp.where(
                is_root, own[block_rows(core, block), cut], relayed
            )
            onward(step, piece).start()
        across(step - 1).start()
        return carry

    lax.fori_loop(1, steps, forward, 0)
    for piece in range(PIECES):
        onward(steps - 1, piece).wait_recv()
    across(steps - 1).start()

    def settle(block):
        at = block_rows(core, block)
        out[at, :] = jnp.where(chosen, came[block + table[2 + core]], own[at, :])

    each(blocks, settle)
    each(steps, lambda step: across(step).wait_recv())

    def settle_other(block):
        at = block_rows(1 - core, block)
        out[at, :] = jnp.where(chosen, mirror[block + table[3 - core]], own[at, :])

    each(blocks, settle_other)
    for piece in range(PIECES):
        onward(steps - 2, piece).wait_send()
        onward(steps - 1, piece).wait_send()
    each(blocks, lambda block: lend(block).wait_send())
    each(steps, lambda step: across(step).wait_send())


def spread(value, table, members, turn, part, parts):
    rows, whole_cols = value.shape
    cols = whole_cols // parts
    height = rows_of(rows, cols, whole_cols)
    blocks = rows // 2 // height
    steps = blocks + members // 2 - 1
    return pl.pallas_call(
        functools.partial(spread_kernel, members, height),
        grid=(1,),
        out_shape=jax.ShapeDtypeStruct((rows, cols), value.dtype),
        in_specs=[
            pl.BlockSpec(memory_space=pltpu.SMEM),
            pl.BlockSpec((rows, cols), lambda i: (0, part), pipeline_mode=pl.Buffered(1)),
        ],
        out_specs=pl.BlockSpec((rows, cols), lambda i: (0, 0), pipeline_mode=pl.Buffered(1)),
        scratch_shapes=[
            pltpu.VMEM((steps, height, cols), value.dtype),
            pltpu.VMEM((steps, height, cols), value.dtype),
            pltpu.VMEM((blocks, height, cols), value.dtype),
            pltpu.VMEM((2, height, cols), value.dtype),
            pltpu.SemaphoreType.DMA((2, PIECES)),
            pltpu.SemaphoreType.DMA((steps, PIECES)),
            pltpu.SemaphoreType.DMA((blocks,)),
            pltpu.SemaphoreType.DMA((blocks,)),
            pltpu.SemaphoreType.DMA((steps,)),
            pltpu.SemaphoreType.DMA((steps,)),
        ],
        compiler_params=pltpu.CompilerParams(
            collective_id=turn, has_side_effects=True, vmem_limit_bytes=60 * 2**20
        ),
        cost_estimate=pl.CostEstimate(
            flops=0, bytes_accessed=300 * 2**20 // parts, transcendentals=0
        ),
        name=f"spread_{turn}",
    )(table, value)


def update_kernel(half, side, rate, turned, mine, theirs, weight, first, second, out):
    block = pl.program_id(0)
    grad = jnp.where(block // half == side[0], mine[...], theirs[...])
    grad_weight = jnp.dot(turned[...], grad, preferred_element_type=jnp.float32)
    momentum = jnp.where(block < half, first[...], second[...]).astype(jnp.float32)
    new_momentum = 0.9 * momentum + grad_weight
    out[...] = (weight[...].astype(jnp.float32) - rate[0] * new_momentum).astype(out.dtype)


def update(side, rate, turned, mine, theirs, weight, first, second):
    rows, cols = weight.shape
    tokens = turned.shape[1]
    half = cols // 2 // TILE
    near = lambda j, side: (0, jnp.clip(j - side[0] * half, 0, half - 1))
    far = lambda j, side: (0, jnp.clip(j - (1 - side[0]) * half, 0, half - 1))
    return pl.pallas_call(
        functools.partial(update_kernel, half),
        grid_spec=pltpu.PrefetchScalarGridSpec(
            num_scalar_prefetch=1,
            grid=(2 * half,),
            in_specs=[
                pl.BlockSpec(memory_space=pltpu.SMEM),
                pl.BlockSpec((rows, tokens), lambda j, side: (0, 0)),
                pl.BlockSpec((tokens, TILE), near),
                pl.BlockSpec((tokens, TILE), far),
                pl.BlockSpec((rows, TILE), lambda j, side: (0, j)),
                pl.BlockSpec((rows, TILE), lambda j, side: (0, jnp.minimum(j, half - 1))),
                pl.BlockSpec((rows, TILE), lambda j, side: (0, jnp.maximum(j - half, 0))),
            ],
            out_specs=pl.BlockSpec((rows, TILE), lambda j, side: (0, j)),
        ),
        out_shape=jax.ShapeDtypeStruct(weight.shape, weight.dtype),
        compiler_params=pltpu.CompilerParams(vmem_limit_bytes=40 * 2**20),
        cost_estimate=pl.CostEstimate(
            flops=2 * rows * cols * tokens,
            bytes_accessed=6 * rows * cols,
            transcendentals=0,
        ),
        name="update",
    )(side, rate, turned, mine, theirs, weight, first, second)


SUB = 128
CHUNK = 256
SPLIT = 2
DEPTH = 6
LAG = 6
LENT = 4
THROTTLE = 8
GRAD_FIRST = 30
FLYING = 2
PACE = 9
LATE = 4
GRAD_EVERY = 2


def fused_kernel(
    members, assign, lr_index, rates, tokens, weight, momentum, cot,
    both, grads, act, turned, late_mine,
    hold, mirror, own, other, taken, theirs, came, mine, again, cot_v, tok_v, turn_v,
    own_sem, lend_send, lend_recv, ring_send, ring_recv, back_send, back_recv,
    x_send, x_recv, g_send, g_recv, out_sem, act_sem, grad_sem, late_sem, again_sem, load_sem,
):
    rows, cols = weight.shape
    half = rows // 2
    part = half // SPLIT
    chunks = cols // CHUNK
    own_chunks = chunks // 2
    per = SPLIT * (CHUNK // SUB)
    all_chunks = 2 * chunks
    units = all_chunks * per
    chips = members // 2
    fill = (chips - 1) * DEPTH
    steps = units + fill
    behind = (fill + LAG) // per
    slots = own.shape[0]

    me = lax.axis_index("pop")
    side = lax.axis_index("tp")
    place = ring_of(me, members)
    chip = place // 2
    core = place % 2
    target = member_at(2 * ((chip + 1 - 2 * core + chips) % chips) + core, members)
    origin = member_at(2 * ((chip - 1 + 2 * core + chips) % chips) + core, members)
    partner = member_at(2 * chip + 1 - core, members)

    root = assign[0, 1]
    root_chip = ring_of(root, members) // 2
    is_root = me == root
    partner_root = partner == root
    chosen = assign[0, 0] == me
    for row in range(1, assign.shape[0]):
        chosen = jnp.logical_or(chosen, assign[row, 0] == me)
    forward_gap = (chip - root_chip + chips) % chips
    backward_gap = (root_chip - chip + chips) % chips
    own_gap = jnp.where(core == 0, forward_gap, backward_gap)
    mirror_gap = jnp.where(core == 0, backward_gap, forward_gap)

    def column(chunk):
        at = chunk % chunks
        first = at < own_chunks
        return jnp.where(first, (1 - side) * own_chunks + at, side * own_chunks + at - own_chunks)

    def half_rows(way, piece):
        return pl.ds(pl.multiple_of(way * half + piece * part, 16), part)

    def load_own(source, chunk):
        cut = pl.ds(pl.multiple_of(column(chunk) * CHUNK, CHUNK), CHUNK)
        slot = chunk % slots
        return pltpu.make_async_copy(source.at[:, cut], own.at[slot], own_sem.at[slot])

    def start_own(chunk):
        @pl.when(chunk < chunks)
        def _():
            load_own(weight, chunk).start()

        @pl.when(chunk >= chunks)
        def _():
            load_own(momentum, chunk).start()

    def lend(chunk):
        away = pl.ds(pl.multiple_of((1 - core) * half, 16), half)
        return pltpu.make_async_remote_copy(
            src_ref=own.at[chunk % slots, away, :],
            dst_ref=other.at[chunk % LENT],
            send_sem=lend_send.at[chunk % LENT],
            recv_sem=lend_recv.at[chunk],
            device_id={"pop": partner},
            device_id_type=MESH,
        )

    def onward(step):
        return pltpu.make_async_remote_copy(
            src_ref=hold.at[step],
            dst_ref=hold.at[step + DEPTH],
            send_sem=ring_send.at[step % THROTTLE],
            recv_sem=ring_recv.at[step + DEPTH],
            device_id={"pop": target},
            device_id_type=MESH,
        )

    def across(step):
        return pltpu.make_async_remote_copy(
            src_ref=hold.at[step],
            dst_ref=mirror.at[step],
            send_sem=back_send.at[step % THROTTLE],
            recv_sem=back_recv.at[step],
            device_id={"pop": partner},
            device_id_type=MESH,
        )

    def trade(piece):
        return pltpu.make_async_remote_copy(
            src_ref=theirs.at[piece],
            dst_ref=came.at[piece],
            send_sem=x_send.at[piece],
            recv_sem=x_recv.at[piece],
            device_id={"tp": 1 - side},
            device_id_type=MESH,
        )

    def trade_grad(piece):
        at = side * own_chunks + piece
        return pltpu.make_async_remote_copy(
            src_ref=mine.at[piece],
            dst_ref=grads.at[at],
            send_sem=g_send.at[piece],
            recv_sem=g_recv.at[piece],
            device_id={"tp": 1 - side},
            device_id_type=MESH,
        )

    def arrived_grad(piece):
        at = (1 - side) * own_chunks + piece
        return pltpu.make_async_remote_copy(
            src_ref=mine.at[piece],
            dst_ref=grads.at[at],
            send_sem=g_send.at[piece],
            recv_sem=g_recv.at[piece],
            device_id={"tp": 1 - side},
            device_id_type=MESH,
        )

    def keep_grad(piece):
        return pltpu.make_async_copy(
            mine.at[piece], grads.at[side * own_chunks + piece], grad_sem.at[piece]
        )

    def keep_late(piece):
        at = piece - (own_chunks - LATE)
        return pltpu.make_async_copy(mine.at[piece], late_mine.at[at], late_sem.at[at])

    def keep_act(piece):
        return pltpu.make_async_copy(came.at[piece], act.at[piece], act_sem.at[piece])

    def keep_taken(chunk):
        place_at = column(chunk) + chunks * (chunk // chunks)
        return pltpu.make_async_copy(
            taken.at[chunk % 3], both.at[place_at], out_sem.at[chunk % 3]
        )

    def fetch_weight(chunk):
        slot = chunk % 2
        return pltpu.make_async_copy(both.at[column(chunk)], again.at[slot], again_sem.at[slot])

    decay = 0.9 * rates[lr_index[me]]
    load_tokens = pltpu.make_async_copy(tokens, tok_v, load_sem.at[0])
    load_cot = pltpu.make_async_copy(cot, cot_v, load_sem.at[1])
    keep_turned = pltpu.make_async_copy(turn_v, turned, load_sem.at[2])

    load_own(weight, 0).start()
    load_tokens.start()
    load_own(weight, 1).start()
    load_own(weight, 2).start()
    load_cot.start()
    barrier = pltpu.get_barrier_semaphore()
    for near in (target, origin, partner):
        pl.semaphore_signal(barrier, inc=1, device_id={"pop": near}, device_id_type=MESH)
    pl.semaphore_signal(barrier, inc=1, device_id={"tp": 1 - side}, device_id_type=MESH)
    pl.semaphore_wait(barrier, 4)
    load_own(weight, 0).wait()
    lend(0).start()
    load_tokens.wait()

    def ring_step(chunk, sub, step):
        piece = sub % SPLIT
        cut = pl.ds((sub // SPLIT) * SUB, SUB)

        @pl.when(jnp.logical_and(step >= DEPTH, step < steps))
        def _():
            onward(step - DEPTH).wait_recv()

        @pl.when(jnp.logical_and(chunk < all_chunks, step < DEPTH))
        def _():
            held = own[chunk % slots, half_rows(core, piece), cut]
            lent = other[chunk % LENT, pl.ds(piece * part, part), cut]
            hold[step] = jnp.where(is_root, held, lent)

        @pl.when(jnp.logical_and(chunk < all_chunks, step >= DEPTH))
        def _():
            held = own[chunk % slots, half_rows(core, piece), cut]
            lent = other[chunk % LENT, pl.ds(piece * part, part), cut]
            hold[step] = jnp.where(is_root, held, jnp.where(partner_root, lent, hold[step]))

        @pl.when(step + DEPTH < steps)
        def _():
            @pl.when(step >= THROTTLE)
            def _():
                onward(step - THROTTLE).wait_send()

            onward(step).start()

        @pl.when(step < steps)
        def _():
            @pl.when(step >= THROTTLE)
            def _():
                across(step - THROTTLE).wait_send()

            across(step).start()

        @pl.when(jnp.logical_and(step >= LAG, step < steps + LAG))
        def _():
            across(step - LAG).wait_recv()

    def consume(chunk, sub):
        piece = sub % SPLIT
        cut = pl.ds((sub // SPLIT) * SUB, SUB)
        unit = chunk * per + sub
        for way, source, gap in ((core, hold, own_gap), (1 - core, mirror, mirror_gap)):
            value = source[unit]
            for hop in range(1, chips):
                value = jnp.where(gap == hop, source[unit + hop * DEPTH], value)
            held = own[chunk % slots, half_rows(way, piece), cut]
            taken[chunk % 3, half_rows(way, piece), cut] = jnp.where(chosen, value, held)

    def finish(chunk):
        @pl.when(chunk < chunks)
        def _():
            value = jnp.dot(
                tok_v[...], taken[chunk % 3], preferred_element_type=jnp.float32
            ).astype(jnp.bfloat16)

            @pl.when(chunk < own_chunks)
            def _():
                theirs[chunk] = value

            @pl.when(chunk >= own_chunks)
            def _():
                mine[chunk - own_chunks] = value

        @pl.when(chunk >= chunks)
        def _():
            fetch_weight(chunk).wait()
            slot = chunk % 3
            tall = 128

            def strip(index, carry):
                at = pl.ds(pl.multiple_of(index * tall, tall), tall)
                kept = again[chunk % 2, at, :].astype(jnp.float32)
                moved = taken[slot, at, :].astype(jnp.float32)
                taken[slot, at, :] = (kept - decay * moved).astype(jnp.bfloat16)
                return carry

            lax.fori_loop(0, rows // tall, strip, 0)

        keep_taken(chunk).start()

    def gradient(piece):
        trade(piece).wait_recv()
        cut = pl.ds(pl.multiple_of(piece * CHUNK, CHUNK), CHUNK)
        tall = 64

        def strip(index, carry):
            at = pl.ds(pl.multiple_of(index * tall, tall), tall)
            value = mine[piece, at, :].astype(jnp.float32) + came[piece, at, :].astype(jnp.float32)
            slope = math.sqrt(2 / math.pi)
            square = value * value
            bent = jnp.tanh(slope * (value + 0.044715 * (square * value)))
            gate = 0.5 * (1.0 + bent)
            rise = 0.5 * value * (1.0 - bent * bent) * (slope * (1.0 + 0.134145 * square))
            came[piece, at, :] = (value * gate).astype(jnp.bfloat16)
            mine[piece, at, :] = (cot_v[at, cut].astype(jnp.float32) * (gate + rise)).astype(
                jnp.bfloat16
            )
            return carry

        lax.fori_loop(0, tok_v.shape[0] // tall, strip, 0)
        keep_grad(piece).start()
        keep_act(piece).start()

        @pl.when(piece >= own_chunks - LATE)
        def _():
            keep_late(piece).start()

    def send_piece(piece):
        @pl.when(piece < own_chunks)
        def _():
            trade(piece).start()

        @pl.when(piece >= own_chunks)
        def _():
            trade_grad(piece - own_chunks).start()

    def sent_piece(piece):
        @pl.when(piece < own_chunks)
        def _():
            trade(piece).wait_send()

        @pl.when(piece >= own_chunks)
        def _():
            trade_grad(piece - own_chunks).wait_send()

    def issue(piece):
        @pl.when(piece >= FLYING)
        def _():
            sent_piece(piece - FLYING)

        send_piece(piece)

    pace_from = (behind + 1) * per
    pieces = 2 * own_chunks - LATE
    in_loop = min(pieces, ((all_chunks + behind) * per - 1 - pace_from) // PACE + 1)

    def turn(chunk, carry):
        @pl.when(chunk < all_chunks)
        def _():
            @pl.when(chunk >= LENT - 1)
            def _():
                lend(chunk - LENT + 1).wait_send()

            @pl.when(chunk + 1 < all_chunks)
            def _():
                load_own(weight, chunk + 1).wait()
                lend(chunk + 1).start()

            @pl.when(chunk + 3 < all_chunks)
            def _():
                start_own(chunk + 3)

            lend(chunk).wait_recv()

        late = chunk - behind

        @pl.when(late >= 3)
        def _():
            keep_taken(late - 3).wait()

        @pl.when(jnp.logical_and(late >= chunks, late < all_chunks))
        def _():
            fetch_weight(late).start()

        for sub in range(per):
            ring_step(chunk, sub, chunk * per + sub)

            @pl.when(late >= 0)
            def _():
                consume(late, sub)

            paced = chunk * per + sub - pace_from

            @pl.when(
                jnp.logical_and(
                    paced >= 0,
                    jnp.logical_and(paced % PACE == 0, paced // PACE < in_loop),
                )
            )
            def _():
                issue(paced // PACE)

        @pl.when(late >= 0)
        def _():
            finish(late)

        @pl.when(chunk == 2)
        def _():
            turn_v[...] = tok_v[...].T
            keep_turned.start()

        @pl.when(chunk == GRAD_FIRST - 1)
        def _():
            load_cot.wait()

        since = chunk - GRAD_FIRST

        @pl.when(
            jnp.logical_and(
                since >= 0,
                jnp.logical_and(since % GRAD_EVERY == 0, since // GRAD_EVERY < own_chunks),
            )
        )
        def _():
            gradient(since // GRAD_EVERY)

        return carry

    lax.fori_loop(0, all_chunks + behind, turn, 0)

    for step in range(steps - DEPTH - THROTTLE, steps - DEPTH):
        onward(step).wait_send()
    for step in range(steps - THROTTLE, steps):
        across(step).wait_send()
    for chunk in range(all_chunks - LENT + 1, all_chunks):
        lend(chunk).wait_send()
    for chunk in range(all_chunks - 3, all_chunks):
        keep_taken(chunk).wait()
    keep_turned.wait()

    def rest(piece, carry):
        issue(piece)
        return carry

    lax.fori_loop(in_loop, pieces, rest, 0)
    for piece in range(pieces - FLYING, pieces):
        sent_piece(piece)

    def drain(piece, carry):
        keep_act(piece).wait()
        keep_grad(piece).wait()

        @pl.when(piece < own_chunks - LATE)
        def _():
            arrived_grad(piece).wait_recv()

        @pl.when(piece >= own_chunks - LATE)
        def _():
            keep_late(piece).wait()

        return carry

    lax.fori_loop(0, own_chunks, drain, 0)


def fused(assignment, lr_index, rates, tokens, weight, momentum, cot, members):
    rows, cols = weight.shape
    count, share = cot.shape
    chunks = cols // CHUNK
    own_chunks = chunks // 2
    per = SPLIT * (CHUNK // SUB)
    chips = members // 2
    fill = (chips - 1) * DEPTH
    steps = 2 * chunks * per + fill
    slots = (fill + LAG) // per + 4
    part = rows // 2 // SPLIT
    kind = weight.dtype
    dma = pltpu.SemaphoreType.DMA
    anywhere = pl.BlockSpec(memory_space=pl.ANY)
    return pl.pallas_call(
        functools.partial(fused_kernel, members),
        out_shape=(
            jax.ShapeDtypeStruct((2 * chunks, rows, CHUNK), kind),
            jax.ShapeDtypeStruct((chunks, count, CHUNK), kind),
            jax.ShapeDtypeStruct((own_chunks, count, CHUNK), kind),
            jax.ShapeDtypeStruct((rows, count), kind),
            jax.ShapeDtypeStruct((LATE, count, CHUNK), kind),
        ),
        in_specs=[pl.BlockSpec(memory_space=pltpu.SMEM)] * 3 + [anywhere] * 4,
        out_specs=(anywhere,) * 5,
        scratch_shapes=[
            pltpu.VMEM((steps, part, SUB), kind),
            pltpu.VMEM((steps, part, SUB), kind),
            pltpu.VMEM((slots, rows, CHUNK), kind),
            pltpu.VMEM((LENT, rows // 2, CHUNK), kind),
            pltpu.VMEM((3, rows, CHUNK), kind),
            pltpu.VMEM((own_chunks, count, CHUNK), kind),
            pltpu.VMEM((own_chunks, count, CHUNK), kind),
            pltpu.VMEM((own_chunks, count, CHUNK), kind),
            pltpu.VMEM((2, rows, CHUNK), kind),
            pltpu.VMEM((count, share), kind),
            pltpu.VMEM((count, rows), kind),
            pltpu.VMEM((rows, count), kind),
            dma((slots,)),
            dma((LENT,)),
            dma((2 * chunks,)),
            dma((THROTTLE,)),
            dma((steps,)),
            dma((THROTTLE,)),
            dma((steps,)),
            dma((own_chunks,)),
            dma((own_chunks,)),
            dma((own_chunks,)),
            dma((own_chunks,)),
            dma((3,)),
            dma((own_chunks,)),
            dma((own_chunks,)),
            dma((LATE,)),
            dma((2,)),
            dma((3,)),
        ],
        compiler_params=pltpu.CompilerParams(
            collective_id=0, has_side_effects=True, vmem_limit_bytes=60 * 2**20
        ),
        name="fused",
    )(assignment, lr_index, rates, tokens, weight, momentum, cot)


def settle_kernel(lr_index, rates, turned, base, grads, *rest):
    out = rest[-2] if len(rest) == 3 else rest[-1]
    rate = rates[lr_index[lax.axis_index("pop")]]
    grad_weight = jnp.dot(turned[...], grads[0], preferred_element_type=jnp.float32)
    out[...] = (base[0].astype(jnp.float32) - rate * grad_weight).astype(out.dtype)
    if len(rest) == 3:
        rest[2][...] = rest[0][0]


def settle(lr_index, rates, turned, both, grads, act):
    rows, count = turned.shape
    chunks = both.shape[0] // 2
    own_chunks = act.shape[0]
    scalar = pl.BlockSpec(memory_space=pltpu.SMEM)

    def column(step):
        side = lax.axis_index("tp")
        far = step >= own_chunks
        return jnp.where(far, (1 - side) * own_chunks + step - own_chunks, side * own_chunks + step)

    return pl.pallas_call(
        settle_kernel,
        grid=(chunks - LATE,),
        in_specs=[
            scalar,
            scalar,
            pl.BlockSpec((rows, count), lambda j: (0, 0)),
            pl.BlockSpec((1, rows, CHUNK), lambda j: (column(j) + chunks, 0, 0)),
            pl.BlockSpec((1, count, CHUNK), lambda j: (column(j), 0, 0)),
            pl.BlockSpec((1, count, CHUNK), lambda j: (jnp.minimum(j, own_chunks - 1), 0, 0)),
        ],
        out_specs=(
            pl.BlockSpec((rows, CHUNK), lambda j: (0, column(j))),
            pl.BlockSpec((count, CHUNK), lambda j: (0, jnp.minimum(j, own_chunks - 1))),
        ),
        out_shape=(
            jax.ShapeDtypeStruct((rows, chunks * CHUNK), both.dtype),
            jax.ShapeDtypeStruct((count, own_chunks * CHUNK), both.dtype),
        ),
        compiler_params=pltpu.CompilerParams(vmem_limit_bytes=60 * 2**20),
        cost_estimate=pl.CostEstimate(
            flops=2 * rows * count * chunks * CHUNK,
            bytes_accessed=6 * rows * chunks * CHUNK,
            transcendentals=0,
        ),
        name="settle",
    )(lr_index, rates, turned, both, grads, act)


def finish_late(lr_index, rates, turned, both, came, partly):
    rows, count = turned.shape
    chunks = both.shape[0] // 2
    own_chunks = chunks // 2
    scalar = pl.BlockSpec(memory_space=pltpu.SMEM)

    def column(step):
        side = lax.axis_index("tp")
        return (1 - side) * own_chunks + own_chunks - LATE + step

    return pl.pallas_call(
        settle_kernel,
        grid=(LATE,),
        in_specs=[
            scalar,
            scalar,
            pl.BlockSpec((rows, count), lambda j: (0, 0)),
            pl.BlockSpec((1, rows, CHUNK), lambda j: (column(j) + chunks, 0, 0)),
            pl.BlockSpec((1, count, CHUNK), lambda j: (j, 0, 0)),
            pl.BlockSpec(memory_space=pl.ANY),
        ],
        out_specs=pl.BlockSpec((rows, CHUNK), lambda j: (0, column(j))),
        out_shape=jax.ShapeDtypeStruct(partly.shape, partly.dtype),
        input_output_aliases={5: 0},
        compiler_params=pltpu.CompilerParams(vmem_limit_bytes=60 * 2**20),
        cost_estimate=pl.CostEstimate(
            flops=2 * rows * count * LATE * CHUNK,
            bytes_accessed=6 * rows * LATE * CHUNK,
            transcendentals=0,
        ),
        name="finish_late",
    )(lr_index, rates, turned, both, came, partly)


def local(tokens, weight, momentum, cotangent, assignment, lr_index, rates):
    members = lax.axis_size("pop")
    ranks = lax.axis_size("tp")
    me = lax.axis_index("pop")
    side = lax.axis_index("tp")
    if ranks == 2 and assignment.shape[0] // 4 == 1:
        both, grads, act, turned, late_mine = fused(
            assignment, lr_index, rates, tokens[0], weight[0], momentum[0], cotangent[0], members
        )
        late_theirs = lax.ppermute(late_mine, "tp", [(0, 1), (1, 0)])
        partly, active = settle(lr_index, rates, turned, both, grads, act)
        late_theirs, partly = lax.optimization_barrier((late_theirs, partly))
        updated = finish_late(lr_index, rates, turned, both, late_theirs, partly)
        return (active[None], updated[None])
    member_ids = jnp.arange(members, dtype=jnp.int32)
    hit = assignment[:, 0] == me
    my_source = jnp.where(jnp.any(hit), jnp.sum(jnp.where(hit, assignment[:, 1], 0)), me)
    my_index = jnp.sum(jnp.where(member_ids == me, lr_index, 0))
    rate_ids = jnp.arange(rates.shape[0], dtype=jnp.int32)
    my_rate = jnp.sum(jnp.where(rate_ids == my_index, rates, 0.0))
    tops = assignment.shape[0] // 4
    winner_hit = assignment[:, 1][None, :] == member_ids[:, None]
    present = jnp.any(winner_hit, axis=1)
    roots = jnp.sort(jnp.where(present, member_ids, members))[:tops]
    place = ring_of(me, members)
    tables = []
    for turn in range(tops):
        root = roots[turn]
        chips = members // 2
        root_place = ring_of(root, members)
        behind = (place // 2 - root_place // 2 + chips) % chips
        entries = (
            me == root,
            jnp.logical_and(my_source == root, me != root),
            (behind + chips - 1) % chips,
            (2 * chips - behind - 1) % chips,
            jnp.logical_and(place // 2 == root_place // 2, me != root),
        )
        tables.append(jnp.stack([entry.astype(jnp.int32) for entry in entries]))

    def take(value, first, part=0, parts=1):
        taken = None
        for turn in range(tops):
            arrived = spread(value, tables[turn], members, first + turn, part, parts)
            if taken is None:
                taken = arrived
            else:
                taken = jnp.where(my_source == roots[turn], arrived, taken)
        return taken

    inputs = tokens[0]
    share_cols = cotangent.shape[2]
    taken_weight = take(weight[0], 0)
    partial_value = jnp.dot(inputs, taken_weight, preferred_element_type=jnp.float32)
    partial_value = partial_value.astype(jnp.bfloat16)
    if ranks == 2:
        swap = [(0, 1), (1, 0)]
        left, right = partial_value[:, :share_cols], partial_value[:, share_cols:]
        mine = jnp.where(side == 0, left, right)
        theirs = jnp.where(side == 0, right, left)
        theirs, raw_momentum = lax.optimization_barrier((theirs, momentum[0]))
        arrived = lax.ppermute(theirs, "tp", swap)
        first = take(raw_momentum, tops, 0, 2)
        arrived, first = lax.optimization_barrier((arrived, first))
        hidden = mine.astype(jnp.float32) + arrived.astype(jnp.float32)
        active, grad_mine = activate(hidden, cotangent[0])
        grad_mine, raw_momentum = lax.optimization_barrier((grad_mine, raw_momentum))
        grad_theirs = lax.ppermute(grad_mine, "tp", swap)
        second = take(raw_momentum, 2 * tops, 1, 2)
        updated = update(
            side.astype(jnp.int32).reshape(1),
            my_rate.reshape(1),
            inputs.T,
            grad_mine,
            grad_theirs,
            taken_weight,
            first,
            second,
        )
    else:
        taken_momentum = take(momentum[0], tops)
        hidden = lax.psum_scatter(
            partial_value, "tp", scatter_dimension=1, tiled=True
        ).astype(jnp.float32)
        active, grad_mine = activate(hidden, cotangent[0])
        grad_hidden = lax.all_gather(grad_mine, "tp", axis=1, tiled=True)
        grad_weight = lax.dot_general(
            inputs, grad_hidden, (((0,), (0,)), ((), ())), preferred_element_type=jnp.float32
        )
        new_momentum = 0.9 * taken_momentum.astype(jnp.float32) + grad_weight
        updated = taken_weight.astype(jnp.float32) - my_rate * new_momentum
        updated = updated.astype(jnp.bfloat16)
    return (active[None], updated[None])


def solution(mesh):
    placed = (
        P("pop", None, "tp"),
        P("pop", "tp", None),
        P("pop", "tp", None),
        P("pop", None, "tp"),
        P(),
        P(),
        P(),
    )
    return jax.shard_map(
        local,
        mesh=mesh,
        in_specs=placed,
        out_specs=(P("pop", None, "tp"), P("pop", "tp", None)),
        check_vma=False,
    )
```

```python
import functools
import math

import jax
import jax.numpy as jnp
from jax import lax
from jax.experimental import pallas as pl
from jax.experimental.pallas import tpu as pltpu
from jax.sharding import PartitionSpec as P

MESH = pl.DeviceIdType.MESH
PIECES = 4
TILE = 512


def ring_of(member, members):
    core = member % 2
    y = (member // 2) % 2
    z = member // 4
    half = members // 4
    chip = z * (1 - y) + (2 * half - 1 - z) * y
    return 2 * chip + core


def member_at(place, members):
    core = place % 2
    chip = place // 2
    half = members // 4
    y = chip // half
    z = chip * (1 - y) + (2 * half - 1 - chip) * y
    return (2 * z + y) * 2 + core


def gelu_tanh(value):
    return jax.nn.gelu(value, approximate=True)


def activate(hidden, cot_block):
    active, pullback = jax.vjp(gelu_tanh, hidden)
    grad_hidden = pullback(cot_block.astype(jnp.float32))[0].astype(jnp.bfloat16)
    return (active.astype(jnp.bfloat16), grad_hidden)


def rows_of(rows, cols, whole_cols):
    wanted = 16 * (whole_cols // cols)
    return wanted if (rows // 2) % wanted == 0 else 16


def spread_kernel(
    members, height, table, own, out, came, mirror, other, sent,
    send_sem, recv_sem, near_send, near_recv, back_send, back_recv,
):
    rows, cols = own.shape
    half = rows // 2
    blocks = half // height
    chips = members // 2
    steps = blocks + chips - 1
    width = cols // PIECES
    place = ring_of(lax.axis_index("pop"), members)
    chip = place // 2
    core = place % 2
    target = member_at(2 * ((chip + 1 - 2 * core + chips) % chips) + core, members)
    origin = member_at(2 * ((chip - 1 + 2 * core + chips) % chips) + core, members)
    partner = member_at(2 * chip + 1 - core, members)
    is_root = table[0] > 0
    chosen = table[1] > 0
    partner_root = table[4] > 0

    barrier = pltpu.get_barrier_semaphore()
    for near in (target, origin, partner):
        pl.semaphore_signal(barrier, inc=1, device_id={"pop": near}, device_id_type=MESH)
    pl.semaphore_wait(barrier, 3)

    def block_rows(way, block):
        return pl.ds(pl.multiple_of(way * half + block * height, height), height)

    def lend(block):
        return pltpu.make_async_remote_copy(
            src_ref=own.at[block_rows(1 - core, block), :],
            dst_ref=other.at[block],
            send_sem=near_send.at[block],
            recv_sem=near_recv.at[block],
            device_id={"pop": partner},
            device_id_type=MESH,
        )

    def onward(step, piece):
        cut = pl.ds(piece * width, width)
        return pltpu.make_async_remote_copy(
            src_ref=sent.at[step % 2, :, cut],
            dst_ref=came.at[step, :, cut],
            send_sem=send_sem.at[step % 2, piece],
            recv_sem=recv_sem.at[step, piece],
            device_id={"pop": target},
            device_id_type=MESH,
        )

    def across(step):
        return pltpu.make_async_remote_copy(
            src_ref=came.at[step],
            dst_ref=mirror.at[step],
            send_sem=back_send.at[step],
            recv_sem=back_recv.at[step],
            device_id={"pop": partner},
            device_id_type=MESH,
        )

    def each(count, act):
        def body(index, carry):
            act(index)
            return carry

        lax.fori_loop(0, count, body, 0)

    each(blocks, lambda block: lend(block).start())
    lend(0).wait_recv()
    for piece in range(PIECES):
        cut = pl.ds(piece * width, width)
        sent[0, :, cut] = jnp.where(is_root, own[block_rows(core, 0), cut], other[0, :, cut])
        onward(0, piece).start()

    def forward(step, carry):
        block = jnp.minimum(step, blocks - 1)

        @pl.when(step < blocks)
        def _():
            lend(step).wait_recv()

        for piece in range(PIECES):
            cut = pl.ds(piece * width, width)
            onward(step - 1, piece).wait_recv()

            @pl.when(step >= 2)
            def _():
                onward(step - 2, piece).wait_send()

            relayed = jnp.where(partner_root, other[block, :, cut], came[step - 1, :, cut])
            sent[step % 2, :, cut] = jnp.where(
                is_root, own[block_rows(core, block), cut], relayed
            )
            onward(step, piece).start()
        across(step - 1).start()
        return carry

    lax.fori_loop(1, steps, forward, 0)
    for piece in range(PIECES):
        onward(steps - 1, piece).wait_recv()
    across(steps - 1).start()

    def settle(block):
        at = block_rows(core, block)
        out[at, :] = jnp.where(chosen, came[block + table[2 + core]], own[at, :])

    each(blocks, settle)
    each(steps, lambda step: across(step).wait_recv())

    def settle_other(block):
        at = block_rows(1 - core, block)
        out[at, :] = jnp.where(chosen, mirror[block + table[3 - core]], own[at, :])

    each(blocks, settle_other)
    for piece in range(PIECES):
        onward(steps - 2, piece).wait_send()
        onward(steps - 1, piece).wait_send()
    each(blocks, lambda block: lend(block).wait_send())
    each(steps, lambda step: across(step).wait_send())


def spread(value, table, members, turn, part, parts):
    rows, whole_cols = value.shape
    cols = whole_cols // parts
    height = rows_of(rows, cols, whole_cols)
    blocks = rows // 2 // height
    steps = blocks + members // 2 - 1
    return pl.pallas_call(
        functools.partial(spread_kernel, members, height),
        grid=(1,),
        out_shape=jax.ShapeDtypeStruct((rows, cols), value.dtype),
        in_specs=[
            pl.BlockSpec(memory_space=pltpu.SMEM),
            pl.BlockSpec((rows, cols), lambda i: (0, part), pipeline_mode=pl.Buffered(1)),
        ],
        out_specs=pl.BlockSpec((rows, cols), lambda i: (0, 0), pipeline_mode=pl.Buffered(1)),
        scratch_shapes=[
            pltpu.VMEM((steps, height, cols), value.dtype),
            pltpu.VMEM((steps, height, cols), value.dtype),
            pltpu.VMEM((blocks, height, cols), value.dtype),
            pltpu.VMEM((2, height, cols), value.dtype),
            pltpu.SemaphoreType.DMA((2, PIECES)),
            pltpu.SemaphoreType.DMA((steps, PIECES)),
            pltpu.SemaphoreType.DMA((blocks,)),
            pltpu.SemaphoreType.DMA((blocks,)),
            pltpu.SemaphoreType.DMA((steps,)),
            pltpu.SemaphoreType.DMA((steps,)),
        ],
        compiler_params=pltpu.CompilerParams(
            collective_id=turn, has_side_effects=True, vmem_limit_bytes=60 * 2**20
        ),
        cost_estimate=pl.CostEstimate(
            flops=0, bytes_accessed=300 * 2**20 // parts, transcendentals=0
        ),
        name=f"spread_{turn}",
    )(table, value)


def update_kernel(half, side, rate, turned, mine, theirs, weight, first, second, out):
    block = pl.program_id(0)
    grad = jnp.where(block // half == side[0], mine[...], theirs[...])
    grad_weight = jnp.dot(turned[...], grad, preferred_element_type=jnp.float32)
    momentum = jnp.where(block < half, first[...], second[...]).astype(jnp.float32)
    new_momentum = 0.9 * momentum + grad_weight
    out[...] = (weight[...].astype(jnp.float32) - rate[0] * new_momentum).astype(out.dtype)


def update(side, rate, turned, mine, theirs, weight, first, second):
    rows, cols = weight.shape
    tokens = turned.shape[1]
    half = cols // 2 // TILE
    near = lambda j, side: (0, jnp.clip(j - side[0] * half, 0, half - 1))
    far = lambda j, side: (0, jnp.clip(j - (1 - side[0]) * half, 0, half - 1))
    return pl.pallas_call(
        functools.partial(update_kernel, half),
        grid_spec=pltpu.PrefetchScalarGridSpec(
            num_scalar_prefetch=1,
            grid=(2 * half,),
            in_specs=[
                pl.BlockSpec(memory_space=pltpu.SMEM),
                pl.BlockSpec((rows, tokens), lambda j, side: (0, 0)),
                pl.BlockSpec((tokens, TILE), near),
                pl.BlockSpec((tokens, TILE), far),
                pl.BlockSpec((rows, TILE), lambda j, side: (0, j)),
                pl.BlockSpec((rows, TILE), lambda j, side: (0, jnp.minimum(j, half - 1))),
                pl.BlockSpec((rows, TILE), lambda j, side: (0, jnp.maximum(j - half, 0))),
            ],
            out_specs=pl.BlockSpec((rows, TILE), lambda j, side: (0, j)),
        ),
        out_shape=jax.ShapeDtypeStruct(weight.shape, weight.dtype),
        compiler_params=pltpu.CompilerParams(vmem_limit_bytes=40 * 2**20),
        cost_estimate=pl.CostEstimate(
            flops=2 * rows * cols * tokens,
            bytes_accessed=6 * rows * cols,
            transcendentals=0,
        ),
        name="update",
    )(side, rate, turned, mine, theirs, weight, first, second)


SUB = 128
CHUNK = 256
SPLIT = 2
DEPTH = 5
LAG = 5
LENT = 4
THROTTLE = 8
GRAD_FIRST = 30
FLYING = 2
PACE = 9
LATE = 3
GRAD_EVERY = 2


def fused_kernel(
    members, assign, lr_index, rates, tokens, weight, momentum, cot,
    both, grads, act, turned, late_mine,
    hold, mirror, own, other, taken, theirs, came, mine, again, cot_v, tok_v, turn_v,
    own_sem, lend_send, lend_recv, ring_send, ring_recv, back_send, back_recv,
    x_send, x_recv, g_send, g_recv, out_sem, act_sem, grad_sem, late_sem, again_sem, load_sem,
):
    rows, cols = weight.shape
    half = rows // 2
    part = half // SPLIT
    chunks = cols // CHUNK
    own_chunks = chunks // 2
    per = SPLIT * (CHUNK // SUB)
    all_chunks = 2 * chunks
    units = all_chunks * per
    chips = members // 2
    fill = (chips - 1) * DEPTH
    steps = units + fill
    behind = (fill + LAG) // per
    slots = own.shape[0]

    me = lax.axis_index("pop")
    side = lax.axis_index("tp")
    place = ring_of(me, members)
    chip = place // 2
    core = place % 2
    target = member_at(2 * ((chip + 1 - 2 * core + chips) % chips) + core, members)
    origin = member_at(2 * ((chip - 1 + 2 * core + chips) % chips) + core, members)
    partner = member_at(2 * chip + 1 - core, members)

    root = assign[1, 0]
    root_chip = ring_of(root, members) // 2
    is_root = me == root
    partner_root = partner == root
    chosen = assign[0, 0] == me
    for row in range(1, assign.shape[1]):
        chosen = jnp.logical_or(chosen, assign[0, row] == me)
    forward_gap = (chip - root_chip + chips) % chips
    backward_gap = (root_chip - chip + chips) % chips
    own_gap = jnp.where(core == 0, forward_gap, backward_gap)
    mirror_gap = jnp.where(core == 0, backward_gap, forward_gap)

    def column(chunk):
        at = chunk % chunks
        first = at < own_chunks
        return jnp.where(first, (1 - side) * own_chunks + at, side * own_chunks + at - own_chunks)

    def half_rows(way, piece):
        return pl.ds(pl.multiple_of(way * half + piece * part, 16), part)

    def load_own(source, chunk):
        cut = pl.ds(pl.multiple_of(column(chunk) * CHUNK, CHUNK), CHUNK)
        slot = chunk % slots
        return pltpu.make_async_copy(source.at[:, cut], own.at[slot], own_sem.at[slot])

    def start_own(chunk):
        @pl.when(chunk < chunks)
        def _():
            load_own(weight, chunk).start()

        @pl.when(chunk >= chunks)
        def _():
            load_own(momentum, chunk).start()

    def lend(chunk):
        away = pl.ds(pl.multiple_of((1 - core) * half, 16), half)
        return pltpu.make_async_remote_copy(
            src_ref=own.at[chunk % slots, away, :],
            dst_ref=other.at[chunk % LENT],
            send_sem=lend_send.at[chunk % LENT],
            recv_sem=lend_recv.at[chunk],
            device_id={"pop": partner},
            device_id_type=MESH,
        )

    def onward(step):
        return pltpu.make_async_remote_copy(
            src_ref=hold.at[step],
            dst_ref=hold.at[step + DEPTH],
            send_sem=ring_send.at[step % THROTTLE],
            recv_sem=ring_recv.at[step + DEPTH],
            device_id={"pop": target},
            device_id_type=MESH,
        )

    def across(step):
        return pltpu.make_async_remote_copy(
            src_ref=hold.at[step],
            dst_ref=mirror.at[step],
            send_sem=back_send.at[step % THROTTLE],
            recv_sem=back_recv.at[step],
            device_id={"pop": partner},
            device_id_type=MESH,
        )

    def trade(piece):
        return pltpu.make_async_remote_copy(
            src_ref=theirs.at[piece],
            dst_ref=came.at[piece],
            send_sem=x_send.at[piece],
            recv_sem=x_recv.at[piece],
            device_id={"tp": 1 - side},
            device_id_type=MESH,
        )

    def trade_grad(piece):
        at = side * own_chunks + piece
        return pltpu.make_async_remote_copy(
            src_ref=mine.at[piece],
            dst_ref=grads.at[at],
            send_sem=g_send.at[piece],
            recv_sem=g_recv.at[piece],
            device_id={"tp": 1 - side},
            device_id_type=MESH,
        )

    def arrived_grad(piece):
        at = (1 - side) * own_chunks + piece
        return pltpu.make_async_remote_copy(
            src_ref=mine.at[piece],
            dst_ref=grads.at[at],
            send_sem=g_send.at[piece],
            recv_sem=g_recv.at[piece],
            device_id={"tp": 1 - side},
            device_id_type=MESH,
        )

    def keep_grad(piece):
        return pltpu.make_async_copy(
            mine.at[piece], grads.at[side * own_chunks + piece], grad_sem.at[piece]
        )

    def keep_late(piece):
        at = piece - (own_chunks - LATE)
        return pltpu.make_async_copy(mine.at[piece], late_mine.at[at], late_sem.at[at])

    def keep_act(piece):
        return pltpu.make_async_copy(came.at[piece], act.at[piece], act_sem.at[piece])

    def keep_taken(chunk):
        place_at = column(chunk) + chunks * (chunk // chunks)
        return pltpu.make_async_copy(
            taken.at[chunk % 3], both.at[place_at], out_sem.at[chunk % 3]
        )

    def fetch_weight(chunk):
        slot = chunk % 2
        return pltpu.make_async_copy(both.at[column(chunk)], again.at[slot], again_sem.at[slot])

    decay = 0.9 * rates[lr_index[me]]
    load_tokens = pltpu.make_async_copy(tokens, tok_v, load_sem.at[0])
    load_cot = pltpu.make_async_copy(cot, cot_v, load_sem.at[1])
    keep_turned = pltpu.make_async_copy(turn_v, turned, load_sem.at[2])

    load_own(weight, 0).start()
    load_tokens.start()
    load_own(weight, 1).start()
    load_own(weight, 2).start()
    load_cot.start()
    barrier = pltpu.get_barrier_semaphore()
    for near in (target, origin, partner):
        pl.semaphore_signal(barrier, inc=1, device_id={"pop": near}, device_id_type=MESH)
    pl.semaphore_signal(barrier, inc=1, device_id={"tp": 1 - side}, device_id_type=MESH)
    pl.semaphore_wait(barrier, 4)
    load_own(weight, 0).wait()
    lend(0).start()
    load_tokens.wait()

    def ring_step(chunk, sub, step):
        piece = sub % SPLIT
        cut = pl.ds((sub // SPLIT) * SUB, SUB)

        @pl.when(jnp.logical_and(step >= DEPTH, step < steps))
        def _():
            onward(step - DEPTH).wait_recv()

        @pl.when(jnp.logical_and(chunk < all_chunks, step < DEPTH))
        def _():
            held = own[chunk % slots, half_rows(core, piece), cut]
            lent = other[chunk % LENT, pl.ds(piece * part, part), cut]
            hold[step] = jnp.where(is_root, held, lent)

        @pl.when(jnp.logical_and(chunk < all_chunks, step >= DEPTH))
        def _():
            held = own[chunk % slots, half_rows(core, piece), cut]
            lent = other[chunk % LENT, pl.ds(piece * part, part), cut]
            hold[step] = jnp.where(is_root, held, jnp.where(partner_root, lent, hold[step]))

        @pl.when(step + DEPTH < steps)
        def _():
            @pl.when(step >= THROTTLE)
            def _():
                onward(step - THROTTLE).wait_send()

            onward(step).start()

        @pl.when(step < steps)
        def _():
            @pl.when(step >= THROTTLE)
            def _():
                across(step - THROTTLE).wait_send()

            across(step).start()

        @pl.when(jnp.logical_and(step >= LAG, step < steps + LAG))
        def _():
            across(step - LAG).wait_recv()

    def consume(chunk, sub):
        piece = sub % SPLIT
        cut = pl.ds((sub // SPLIT) * SUB, SUB)
        unit = chunk * per + sub
        for way, source, gap in ((core, hold, own_gap), (1 - core, mirror, mirror_gap)):
            value = source[unit]
            for hop in range(1, chips):
                value = jnp.where(gap == hop, source[unit + hop * DEPTH], value)
            held = own[chunk % slots, half_rows(way, piece), cut]
            taken[chunk % 3, half_rows(way, piece), cut] = jnp.where(chosen, value, held)

    def finish(chunk):
        @pl.when(chunk < chunks)
        def _():
            value = jnp.dot(
                tok_v[...], taken[chunk % 3], preferred_element_type=jnp.float32
            ).astype(jnp.bfloat16)

            @pl.when(chunk < own_chunks)
            def _():
                theirs[chunk] = value

            @pl.when(chunk >= own_chunks)
            def _():
                mine[chunk - own_chunks] = value

        @pl.when(chunk >= chunks)
        def _():
            fetch_weight(chunk).wait()
            slot = chunk % 3
            tall = 128

            def strip(index, carry):
                at = pl.ds(pl.multiple_of(index * tall, tall), tall)
                kept = again[chunk % 2, at, :].astype(jnp.float32)
                moved = taken[slot, at, :].astype(jnp.float32)
                taken[slot, at, :] = (kept - decay * moved).astype(jnp.bfloat16)
                return carry

            lax.fori_loop(0, rows // tall, strip, 0)

        keep_taken(chunk).start()

    def gradient(piece, sub):
        if sub == 0:
            trade(piece).wait_recv()
        cut = pl.ds(pl.multiple_of(piece * CHUNK, CHUNK), CHUNK)
        tall = 64

        def strip(index, carry):
            at = pl.ds(pl.multiple_of(index * tall, tall), tall)
            value = mine[piece, at, :].astype(jnp.float32) + came[piece, at, :].astype(jnp.float32)
            slope = math.sqrt(2 / math.pi)
            square = value * value
            bent = jnp.tanh(slope * (value + 0.044715 * (square * value)))
            gate = 0.5 * (1.0 + bent)
            rise = 0.5 * value * (1.0 - bent * bent) * (slope * (1.0 + 0.134145 * square))
            came[piece, at, :] = (value * gate).astype(jnp.bfloat16)
            mine[piece, at, :] = (cot_v[at, cut].astype(jnp.float32) * (gate + rise)).astype(
                jnp.bfloat16
            )
            return carry

        strips = tok_v.shape[0] // tall // per
        lax.fori_loop(strips * sub, strips * (sub + 1), strip, 0)
        if sub < per - 1:
            return
        keep_grad(piece).start()
        keep_act(piece).start()

        @pl.when(piece >= own_chunks - LATE)
        def _():
            keep_late(piece).start()

    def send_piece(piece):
        @pl.when(piece < own_chunks)
        def _():
            trade(piece).start()

        @pl.when(piece >= own_chunks)
        def _():
            trade_grad(piece - own_chunks).start()

    def sent_piece(piece):
        @pl.when(piece < own_chunks)
        def _():
            trade(piece).wait_send()

        @pl.when(piece >= own_chunks)
        def _():
            trade_grad(piece - own_chunks).wait_send()

    def issue(piece):
        @pl.when(piece >= FLYING)
        def _():
            sent_piece(piece - FLYING)

        send_piece(piece)

    pace_from = (behind + 1) * per
    pieces = 2 * own_chunks - LATE
    in_loop = min(pieces, ((all_chunks + behind + 1) * per - 1 - pace_from) // PACE + 1)

    def turn(chunk, carry):
        @pl.when(chunk < all_chunks)
        def _():
            @pl.when(chunk >= LENT - 1)
            def _():
                lend(chunk - LENT + 1).wait_send()

            @pl.when(chunk + 1 < all_chunks)
            def _():
                load_own(weight, chunk + 1).wait()
                lend(chunk + 1).start()

            @pl.when(chunk + 3 < all_chunks)
            def _():
                start_own(chunk + 3)

            lend(chunk).wait_recv()

        late = chunk - behind

        @pl.when(jnp.logical_and(late >= 3, late < all_chunks))
        def _():
            keep_taken(late - 3).wait()

        @pl.when(jnp.logical_and(late >= chunks, late < all_chunks))
        def _():
            fetch_weight(late).start()

        for sub in range(per):
            ring_step(chunk, sub, chunk * per + sub)

            @pl.when(jnp.logical_and(late >= 0, late < all_chunks))
            def _():
                consume(late, sub)

            if sub == 0:

                @pl.when(late >= 1)
                def _():
                    finish(late - 1)
            else:
                since = chunk - GRAD_FIRST

                @pl.when(
                    jnp.logical_and(
                        since >= 0,
                        jnp.logical_and(
                            since % GRAD_EVERY == 0, since // GRAD_EVERY < own_chunks
                        ),
                    )
                )
                def _():
                    for part_of in (0, 1) if sub == 1 else (sub,):
                        gradient(since // GRAD_EVERY, part_of)

            paced = chunk * per + sub - pace_from

            @pl.when(
                jnp.logical_and(
                    paced >= 0,
                    jnp.logical_and(paced % PACE == 0, paced // PACE < in_loop),
                )
            )
            def _():
                issue(paced // PACE)

        @pl.when(chunk == 2)
        def _():
            turn_v[...] = tok_v[...].T
            keep_turned.start()

        @pl.when(chunk == GRAD_FIRST - 1)
        def _():
            load_cot.wait()

        return carry

    lax.fori_loop(0, all_chunks + behind + 1, turn, 0)

    for step in range(steps - DEPTH - THROTTLE, steps - DEPTH):
        onward(step).wait_send()
    for step in range(steps - THROTTLE, steps):
        across(step).wait_send()
    for chunk in range(all_chunks - LENT + 1, all_chunks):
        lend(chunk).wait_send()
    for chunk in range(all_chunks - 3, all_chunks):
        keep_taken(chunk).wait()
    keep_turned.wait()

    def rest(piece, carry):
        issue(piece)
        return carry

    lax.fori_loop(in_loop, pieces, rest, 0)
    for piece in range(pieces - FLYING, pieces):
        sent_piece(piece)

    def drain(piece, carry):
        keep_act(piece).wait()
        keep_grad(piece).wait()

        @pl.when(piece < own_chunks - LATE)
        def _():
            arrived_grad(piece).wait_recv()

        @pl.when(piece >= own_chunks - LATE)
        def _():
            keep_late(piece).wait()

        return carry

    lax.fori_loop(0, own_chunks, drain, 0)


def fused(assignment, lr_index, rates, tokens, weight, momentum, cot, members):
    rows, cols = weight.shape
    count, share = cot.shape
    chunks = cols // CHUNK
    own_chunks = chunks // 2
    per = SPLIT * (CHUNK // SUB)
    chips = members // 2
    fill = (chips - 1) * DEPTH
    steps = 2 * chunks * per + fill
    slots = (fill + LAG) // per + 4
    part = rows // 2 // SPLIT
    kind = weight.dtype
    dma = pltpu.SemaphoreType.DMA
    anywhere = pl.BlockSpec(memory_space=pl.ANY)
    return pl.pallas_call(
        functools.partial(fused_kernel, members),
        out_shape=(
            jax.ShapeDtypeStruct((2 * chunks, rows, CHUNK), kind),
            jax.ShapeDtypeStruct((chunks, count, CHUNK), kind),
            jax.ShapeDtypeStruct((own_chunks, count, CHUNK), kind),
            jax.ShapeDtypeStruct((rows, count), kind),
            jax.ShapeDtypeStruct((LATE, count, CHUNK), kind),
        ),
        in_specs=[pl.BlockSpec(memory_space=pltpu.SMEM)] * 3 + [anywhere] * 4,
        out_specs=(anywhere,) * 5,
        scratch_shapes=[
            pltpu.VMEM((steps, part, SUB), kind),
            pltpu.VMEM((steps, part, SUB), kind),
            pltpu.VMEM((slots, rows, CHUNK), kind),
            pltpu.VMEM((LENT, rows // 2, CHUNK), kind),
            pltpu.VMEM((3, rows, CHUNK), kind),
            pltpu.VMEM((own_chunks, count, CHUNK), kind),
            pltpu.VMEM((own_chunks, count, CHUNK), kind),
            pltpu.VMEM((own_chunks, count, CHUNK), kind),
            pltpu.VMEM((2, rows, CHUNK), kind),
            pltpu.VMEM((count, share), kind),
            pltpu.VMEM((count, rows), kind),
            pltpu.VMEM((rows, count), kind),
            dma((slots,)),
            dma((LENT,)),
            dma((2 * chunks,)),
            dma((THROTTLE,)),
            dma((steps,)),
            dma((THROTTLE,)),
            dma((steps,)),
            dma((own_chunks,)),
            dma((own_chunks,)),
            dma((own_chunks,)),
            dma((own_chunks,)),
            dma((3,)),
            dma((own_chunks,)),
            dma((own_chunks,)),
            dma((LATE,)),
            dma((2,)),
            dma((3,)),
        ],
        compiler_params=pltpu.CompilerParams(
            collective_id=0, has_side_effects=True, vmem_limit_bytes=60 * 2**20
        ),
        name="fused",
    )(assignment, lr_index, rates, tokens, weight, momentum, cot)


def settle_kernel(
    column, source, count, lr_index, rates, turned, both, grads, extra, out, *rest
):
    *active, turn_v, base_v, grad_v, act_v, turn_sem, base_sem, grad_sem, out_sem, act_in, act_out = rest
    rows = turned.shape[0]
    chunks = both.shape[0] // 2
    pieces = act_v.shape[0] if active else 0
    rate = rates[lr_index[lax.axis_index("pop")]]

    def load_base(step):
        return pltpu.make_async_copy(
            both.at[chunks + column(step)], base_v.at[step], base_sem.at[step]
        )

    def load_grad(step):
        return pltpu.make_async_copy(grads.at[source(step)], grad_v.at[step], grad_sem.at[step])

    def store(step):
        cut = pl.ds(pl.multiple_of(column(step) * CHUNK, CHUNK), CHUNK)
        return pltpu.make_async_copy(base_v.at[step], out.at[:, cut], out_sem.at[step])

    def load_act(step):
        return pltpu.make_async_copy(extra.at[step], act_v.at[step], act_in.at[step])

    def store_act(step):
        cut = pl.ds(pl.multiple_of(step * CHUNK, CHUNK), CHUNK)
        return pltpu.make_async_copy(act_v.at[step], active[0].at[:, cut], act_out.at[step])

    def each(total, act):
        def body(index, carry):
            act(index)
            return carry

        if total:
            lax.fori_loop(0, total, body, 0)

    load_turned = pltpu.make_async_copy(turned, turn_v, turn_sem.at[0])
    load_turned.start()

    def begin(step):
        load_base(step).start()
        load_grad(step).start()

    each(count, begin)
    each(pieces, lambda step: load_act(step).start())
    load_turned.wait()

    def work(step):
        load_base(step).wait()
        load_grad(step).wait()
        tall = 128
        for top in range(0, rows, tall):
            at = pl.ds(top, tall)
            grad_weight = jnp.dot(
                turn_v[at, :], grad_v[step], preferred_element_type=jnp.float32
            )
            base = base_v[step, at, :].astype(jnp.float32)
            base_v[step, at, :] = (base - rate * grad_weight).astype(base_v.dtype)
        store(step).start()
        if pieces:

            @pl.when(step < pieces)
            def _():
                load_act(step).wait()
                store_act(step).start()

    each(count, work)
    each(count, lambda step: store(step).wait())
    each(pieces, lambda step: store_act(step).wait())


def settle(column, source, count, lr_index, rates, turned, both, grads, act, partly=None):
    rows, tall = turned.shape
    chunks = both.shape[0] // 2
    kind = both.dtype
    scalar = pl.BlockSpec(memory_space=pltpu.SMEM)
    anywhere = pl.BlockSpec(memory_space=pl.ANY)
    dma = pltpu.SemaphoreType.DMA
    pieces = chunks // 2 if partly is None else 1
    whole = jax.ShapeDtypeStruct((rows, chunks * CHUNK), kind)
    if partly is None:
        shapes = (whole, jax.ShapeDtypeStruct((tall, pieces * CHUNK), kind))
    else:
        shapes = whole
    return pl.pallas_call(
        functools.partial(settle_kernel, column, source, count),
        in_specs=[scalar, scalar] + [anywhere] * 4,
        out_specs=(anywhere, anywhere) if partly is None else anywhere,
        out_shape=shapes,
        scratch_shapes=[
            pltpu.VMEM((rows, tall), kind),
            pltpu.VMEM((count, rows, CHUNK), kind),
            pltpu.VMEM((count, tall, CHUNK), kind),
            pltpu.VMEM((pieces, tall, CHUNK), kind),
            dma((1,)),
            dma((count,)),
            dma((count,)),
            dma((count,)),
            dma((pieces,)),
            dma((pieces,)),
        ],
        input_output_aliases={} if partly is None else {5: 0},
        compiler_params=pltpu.CompilerParams(vmem_limit_bytes=60 * 2**20),
        cost_estimate=pl.CostEstimate(
            flops=2 * rows * tall * count * CHUNK,
            bytes_accessed=6 * rows * count * CHUNK,
            transcendentals=0,
        ),
        name="settle" if partly is None else "settle_late",
    )(lr_index, rates, turned, both, grads, act if partly is None else partly)


def local(tokens, weight, momentum, cotangent, assignment, lr_index, rates):
    members = lax.axis_size("pop")
    ranks = lax.axis_size("tp")
    me = lax.axis_index("pop")
    side = lax.axis_index("tp")
    if ranks == 2 and assignment.shape[0] // 4 == 1:
        both, grads, act, turned, late_mine = fused(
            assignment.T, lr_index, rates, tokens[0], weight[0], momentum[0], cotangent[0], members
        )
        late_theirs = lax.ppermute(late_mine, "tp", [(0, 1), (1, 0)])
        own_chunks = act.shape[0]

        def early(step):
            far = step >= own_chunks
            side_of = lax.axis_index("tp")
            return jnp.where(far, (1 - side_of) * own_chunks + step - own_chunks, side_of * own_chunks + step)

        def late(step):
            return (1 - lax.axis_index("tp")) * own_chunks + own_chunks - LATE + step

        partly, active = settle(
            early, early, 2 * own_chunks - LATE, lr_index, rates, turned, both, grads, act
        )
        late_theirs, partly = lax.optimization_barrier((late_theirs, partly))
        updated = settle(
            late, lambda step: step, LATE, lr_index, rates, turned, both, late_theirs, None, partly
        )
        return (active[None], updated[None])
    member_ids = jnp.arange(members, dtype=jnp.int32)
    hit = assignment[:, 0] == me
    my_source = jnp.where(jnp.any(hit), jnp.sum(jnp.where(hit, assignment[:, 1], 0)), me)
    my_index = jnp.sum(jnp.where(member_ids == me, lr_index, 0))
    rate_ids = jnp.arange(rates.shape[0], dtype=jnp.int32)
    my_rate = jnp.sum(jnp.where(rate_ids == my_index, rates, 0.0))
    tops = assignment.shape[0] // 4
    winner_hit = assignment[:, 1][None, :] == member_ids[:, None]
    present = jnp.any(winner_hit, axis=1)
    roots = jnp.sort(jnp.where(present, member_ids, members))[:tops]
    place = ring_of(me, members)
    tables = []
    for turn in range(tops):
        root = roots[turn]
        chips = members // 2
        root_place = ring_of(root, members)
        behind = (place // 2 - root_place // 2 + chips) % chips
        entries = (
            me == root,
            jnp.logical_and(my_source == root, me != root),
            (behind + chips - 1) % chips,
            (2 * chips - behind - 1) % chips,
            jnp.logical_and(place // 2 == root_place // 2, me != root),
        )
        tables.append(jnp.stack([entry.astype(jnp.int32) for entry in entries]))

    def take(value, first, part=0, parts=1):
        taken = None
        for turn in range(tops):
            arrived = spread(value, tables[turn], members, first + turn, part, parts)
            if taken is None:
                taken = arrived
            else:
                taken = jnp.where(my_source == roots[turn], arrived, taken)
        return taken

    inputs = tokens[0]
    share_cols = cotangent.shape[2]
    taken_weight = take(weight[0], 0)
    partial_value = jnp.dot(inputs, taken_weight, preferred_element_type=jnp.float32)
    partial_value = partial_value.astype(jnp.bfloat16)
    if ranks == 2:
        swap = [(0, 1), (1, 0)]
        left, right = partial_value[:, :share_cols], partial_value[:, share_cols:]
        mine = jnp.where(side == 0, left, right)
        theirs = jnp.where(side == 0, right, left)
        theirs, raw_momentum = lax.optimization_barrier((theirs, momentum[0]))
        arrived = lax.ppermute(theirs, "tp", swap)
        first = take(raw_momentum, tops, 0, 2)
        arrived, first = lax.optimization_barrier((arrived, first))
        hidden = mine.astype(jnp.float32) + arrived.astype(jnp.float32)
        active, grad_mine = activate(hidden, cotangent[0])
        grad_mine, raw_momentum = lax.optimization_barrier((grad_mine, raw_momentum))
        grad_theirs = lax.ppermute(grad_mine, "tp", swap)
        second = take(raw_momentum, 2 * tops, 1, 2)
        updated = update(
            side.astype(jnp.int32).reshape(1),
            my_rate.reshape(1),
            inputs.T,
            grad_mine,
            grad_theirs,
            taken_weight,
            first,
            second,
        )
    else:
        taken_momentum = take(momentum[0], tops)
        hidden = lax.psum_scatter(
            partial_value, "tp", scatter_dimension=1, tiled=True
        ).astype(jnp.float32)
        active, grad_mine = activate(hidden, cotangent[0])
        grad_hidden = lax.all_gather(grad_mine, "tp", axis=1, tiled=True)
        grad_weight = lax.dot_general(
            inputs, grad_hidden, (((0,), (0,)), ((), ())), preferred_element_type=jnp.float32
        )
        new_momentum = 0.9 * taken_momentum.astype(jnp.float32) + grad_weight
        updated = taken_weight.astype(jnp.float32) - my_rate * new_momentum
        updated = updated.astype(jnp.bfloat16)
    return (active[None], updated[None])


def solution(mesh):
    placed = (
        P("pop", None, "tp"),
        P("pop", "tp", None),
        P("pop", "tp", None),
        P("pop", None, "tp"),
        P(),
        P(),
        P(),
    )
    return jax.shard_map(
        local,
        mesh=mesh,
        in_specs=placed,
        out_specs=(P("pop", None, "tp"), P("pop", "tp", None)),
        check_vma=False,
    )
```

```python
import functools
import math

import jax
import jax.numpy as jnp
from jax import lax
from jax.experimental import pallas as pl
from jax.experimental.pallas import tpu as pltpu
from jax.sharding import PartitionSpec as P

MESH = pl.DeviceIdType.MESH
PIECES = 4
TILE = 512


def ring_of(member, members):
    core = member % 2
    y = (member // 2) % 2
    z = member // 4
    half = members // 4
    chip = z * (1 - y) + (2 * half - 1 - z) * y
    return 2 * chip + core


def member_at(place, members):
    core = place % 2
    chip = place // 2
    half = members // 4
    y = chip // half
    z = chip * (1 - y) + (2 * half - 1 - chip) * y
    return (2 * z + y) * 2 + core


def gelu_tanh(value):
    return jax.nn.gelu(value, approximate=True)


def activate(hidden, cot_block):
    active, pullback = jax.vjp(gelu_tanh, hidden)
    grad_hidden = pullback(cot_block.astype(jnp.float32))[0].astype(jnp.bfloat16)
    return (active.astype(jnp.bfloat16), grad_hidden)


def rows_of(rows, cols, whole_cols):
    wanted = 16 * (whole_cols // cols)
    return wanted if (rows // 2) % wanted == 0 else 16


def spread_kernel(
    members, height, table, own, out, came, mirror, other, sent,
    send_sem, recv_sem, near_send, near_recv, back_send, back_recv,
):
    rows, cols = own.shape
    half = rows // 2
    blocks = half // height
    chips = members // 2
    steps = blocks + chips - 1
    width = cols // PIECES
    place = ring_of(lax.axis_index("pop"), members)
    chip = place // 2
    core = place % 2
    target = member_at(2 * ((chip + 1 - 2 * core + chips) % chips) + core, members)
    origin = member_at(2 * ((chip - 1 + 2 * core + chips) % chips) + core, members)
    partner = member_at(2 * chip + 1 - core, members)
    is_root = table[0] > 0
    chosen = table[1] > 0
    partner_root = table[4] > 0

    barrier = pltpu.get_barrier_semaphore()
    for near in (target, origin, partner):
        pl.semaphore_signal(barrier, inc=1, device_id={"pop": near}, device_id_type=MESH)
    pl.semaphore_wait(barrier, 3)

    def block_rows(way, block):
        return pl.ds(pl.multiple_of(way * half + block * height, height), height)

    def lend(block):
        return pltpu.make_async_remote_copy(
            src_ref=own.at[block_rows(1 - core, block), :],
            dst_ref=other.at[block],
            send_sem=near_send.at[block],
            recv_sem=near_recv.at[block],
            device_id={"pop": partner},
            device_id_type=MESH,
        )

    def onward(step, piece):
        cut = pl.ds(piece * width, width)
        return pltpu.make_async_remote_copy(
            src_ref=sent.at[step % 2, :, cut],
            dst_ref=came.at[step, :, cut],
            send_sem=send_sem.at[step % 2, piece],
            recv_sem=recv_sem.at[step, piece],
            device_id={"pop": target},
            device_id_type=MESH,
        )

    def across(step):
        return pltpu.make_async_remote_copy(
            src_ref=came.at[step],
            dst_ref=mirror.at[step],
            send_sem=back_send.at[step],
            recv_sem=back_recv.at[step],
            device_id={"pop": partner},
            device_id_type=MESH,
        )

    def each(count, act):
        def body(index, carry):
            act(index)
            return carry

        lax.fori_loop(0, count, body, 0)

    each(blocks, lambda block: lend(block).start())
    lend(0).wait_recv()
    for piece in range(PIECES):
        cut = pl.ds(piece * width, width)
        sent[0, :, cut] = jnp.where(is_root, own[block_rows(core, 0), cut], other[0, :, cut])
        onward(0, piece).start()

    def forward(step, carry):
        block = jnp.minimum(step, blocks - 1)

        @pl.when(step < blocks)
        def _():
            lend(step).wait_recv()

        for piece in range(PIECES):
            cut = pl.ds(piece * width, width)
            onward(step - 1, piece).wait_recv()

            @pl.when(step >= 2)
            def _():
                onward(step - 2, piece).wait_send()

            relayed = jnp.where(partner_root, other[block, :, cut], came[step - 1, :, cut])
            sent[step % 2, :, cut] = jnp.where(
                is_root, own[block_rows(core, block), cut], relayed
            )
            onward(step, piece).start()
        across(step - 1).start()
        return carry

    lax.fori_loop(1, steps, forward, 0)
    for piece in range(PIECES):
        onward(steps - 1, piece).wait_recv()
    across(steps - 1).start()

    def settle(block):
        at = block_rows(core, block)
        out[at, :] = jnp.where(chosen, came[block + table[2 + core]], own[at, :])

    each(blocks, settle)
    each(steps, lambda step: across(step).wait_recv())

    def settle_other(block):
        at = block_rows(1 - core, block)
        out[at, :] = jnp.where(chosen, mirror[block + table[3 - core]], own[at, :])

    each(blocks, settle_other)
    for piece in range(PIECES):
        onward(steps - 2, piece).wait_send()
        onward(steps - 1, piece).wait_send()
    each(blocks, lambda block: lend(block).wait_send())
    each(steps, lambda step: across(step).wait_send())


def spread(value, table, members, turn, part, parts):
    rows, whole_cols = value.shape
    cols = whole_cols // parts
    height = rows_of(rows, cols, whole_cols)
    blocks = rows // 2 // height
    steps = blocks + members // 2 - 1
    return pl.pallas_call(
        functools.partial(spread_kernel, members, height),
        grid=(1,),
        out_shape=jax.ShapeDtypeStruct((rows, cols), value.dtype),
        in_specs=[
            pl.BlockSpec(memory_space=pltpu.SMEM),
            pl.BlockSpec((rows, cols), lambda i: (0, part), pipeline_mode=pl.Buffered(1)),
        ],
        out_specs=pl.BlockSpec((rows, cols), lambda i: (0, 0), pipeline_mode=pl.Buffered(1)),
        scratch_shapes=[
            pltpu.VMEM((steps, height, cols), value.dtype),
            pltpu.VMEM((steps, height, cols), value.dtype),
            pltpu.VMEM((blocks, height, cols), value.dtype),
            pltpu.VMEM((2, height, cols), value.dtype),
            pltpu.SemaphoreType.DMA((2, PIECES)),
            pltpu.SemaphoreType.DMA((steps, PIECES)),
            pltpu.SemaphoreType.DMA((blocks,)),
            pltpu.SemaphoreType.DMA((blocks,)),
            pltpu.SemaphoreType.DMA((steps,)),
            pltpu.SemaphoreType.DMA((steps,)),
        ],
        compiler_params=pltpu.CompilerParams(
            collective_id=turn, has_side_effects=True, vmem_limit_bytes=60 * 2**20
        ),
        cost_estimate=pl.CostEstimate(
            flops=0, bytes_accessed=300 * 2**20 // parts, transcendentals=0
        ),
        name=f"spread_{turn}",
    )(table, value)


def update_kernel(half, side, rate, turned, mine, theirs, weight, first, second, out):
    block = pl.program_id(0)
    grad = jnp.where(block // half == side[0], mine[...], theirs[...])
    grad_weight = jnp.dot(turned[...], grad, preferred_element_type=jnp.float32)
    momentum = jnp.where(block < half, first[...], second[...]).astype(jnp.float32)
    new_momentum = 0.9 * momentum + grad_weight
    out[...] = (weight[...].astype(jnp.float32) - rate[0] * new_momentum).astype(out.dtype)


def update(side, rate, turned, mine, theirs, weight, first, second):
    rows, cols = weight.shape
    tokens = turned.shape[1]
    half = cols // 2 // TILE
    near = lambda j, side: (0, jnp.clip(j - side[0] * half, 0, half - 1))
    far = lambda j, side: (0, jnp.clip(j - (1 - side[0]) * half, 0, half - 1))
    return pl.pallas_call(
        functools.partial(update_kernel, half),
        grid_spec=pltpu.PrefetchScalarGridSpec(
            num_scalar_prefetch=1,
            grid=(2 * half,),
            in_specs=[
                pl.BlockSpec(memory_space=pltpu.SMEM),
                pl.BlockSpec((rows, tokens), lambda j, side: (0, 0)),
                pl.BlockSpec((tokens, TILE), near),
                pl.BlockSpec((tokens, TILE), far),
                pl.BlockSpec((rows, TILE), lambda j, side: (0, j)),
                pl.BlockSpec((rows, TILE), lambda j, side: (0, jnp.minimum(j, half - 1))),
                pl.BlockSpec((rows, TILE), lambda j, side: (0, jnp.maximum(j - half, 0))),
            ],
            out_specs=pl.BlockSpec((rows, TILE), lambda j, side: (0, j)),
        ),
        out_shape=jax.ShapeDtypeStruct(weight.shape, weight.dtype),
        compiler_params=pltpu.CompilerParams(vmem_limit_bytes=40 * 2**20),
        cost_estimate=pl.CostEstimate(
            flops=2 * rows * cols * tokens,
            bytes_accessed=6 * rows * cols,
            transcendentals=0,
        ),
        name="update",
    )(side, rate, turned, mine, theirs, weight, first, second)


SUB = 128
CHUNK = 256
SPLIT = 2
DEPTH = 5
LAG = 5
LENT = 4
THROTTLE = 8
GRAD_FIRST = 30
FLYING = 3
PACE = 17
LATE = 3
LATE_LIMIT = 60
GRAD_EVERY = 2


def fused_kernel(
    members, assign, lr_index, rates, tokens, weight, momentum, cot,
    both, grads, act, turned, late_mine,
    hold, mirror, own, other, taken, theirs, came, mine, again, cot_v, tok_v, turn_v,
    own_sem, lend_send, lend_recv, ring_send, ring_recv, back_send, back_recv,
    x_send, x_recv, g_send, g_recv, out_sem, act_sem, late_sem, again_sem, load_sem,
):
    rows, cols = weight.shape
    half = rows // 2
    part = half // SPLIT
    chunks = cols // CHUNK
    own_chunks = chunks // 2
    per = SPLIT * (CHUNK // SUB)
    all_chunks = 2 * chunks
    units = all_chunks * per
    chips = members // 2
    fill = (chips - 1) * DEPTH
    steps = units + fill
    behind = fill + LAG
    shift = behind % per
    rounds = all_chunks + (behind + per - 1) // per + 1
    slots = own.shape[0]

    me = lax.axis_index("pop")
    side = lax.axis_index("tp")
    place = ring_of(me, members)
    chip = place // 2
    core = place % 2
    target = member_at(2 * ((chip + 1 - 2 * core + chips) % chips) + core, members)
    origin = member_at(2 * ((chip - 1 + 2 * core + chips) % chips) + core, members)
    partner = member_at(2 * chip + 1 - core, members)

    root = assign[1, 0]
    root_chip = ring_of(root, members) // 2
    is_root = me == root
    partner_root = partner == root
    chosen = assign[0, 0] == me
    for row in range(1, assign.shape[1]):
        chosen = jnp.logical_or(chosen, assign[0, row] == me)
    forward_gap = (chip - root_chip + chips) % chips
    backward_gap = (root_chip - chip + chips) % chips
    own_gap = jnp.where(core == 0, forward_gap, backward_gap)
    mirror_gap = jnp.where(core == 0, backward_gap, forward_gap)

    def column(chunk):
        at = chunk % chunks
        first = at < own_chunks
        return jnp.where(first, (1 - side) * own_chunks + at, side * own_chunks + at - own_chunks)

    def half_rows(way, piece):
        return pl.ds(pl.multiple_of(way * half + piece * part, 16), part)

    def load_own(source, chunk):
        cut = pl.ds(pl.multiple_of(column(chunk) * CHUNK, CHUNK), CHUNK)
        slot = chunk % slots
        return pltpu.make_async_copy(source.at[:, cut], own.at[slot], own_sem.at[slot])

    def start_own(chunk):
        @pl.when(chunk < chunks)
        def _():
            load_own(weight, chunk).start()

        @pl.when(chunk >= chunks)
        def _():
            load_own(momentum, chunk).start()

    def lend(chunk):
        away = pl.ds(pl.multiple_of((1 - core) * half, 16), half)
        return pltpu.make_async_remote_copy(
            src_ref=own.at[chunk % slots, away, :],
            dst_ref=other.at[chunk % LENT],
            send_sem=lend_send.at[chunk % LENT],
            recv_sem=lend_recv.at[chunk],
            device_id={"pop": partner},
            device_id_type=MESH,
        )

    def onward(step):
        return pltpu.make_async_remote_copy(
            src_ref=hold.at[step],
            dst_ref=hold.at[step + DEPTH],
            send_sem=ring_send.at[step % THROTTLE],
            recv_sem=ring_recv.at[step + DEPTH],
            device_id={"pop": target},
            device_id_type=MESH,
        )

    def across(step):
        return pltpu.make_async_remote_copy(
            src_ref=hold.at[step],
            dst_ref=mirror.at[step],
            send_sem=back_send.at[step % THROTTLE],
            recv_sem=back_recv.at[step],
            device_id={"pop": partner},
            device_id_type=MESH,
        )

    def trade(piece):
        return pltpu.make_async_remote_copy(
            src_ref=theirs.at[piece],
            dst_ref=came.at[piece],
            send_sem=x_send.at[piece],
            recv_sem=x_recv.at[piece],
            device_id={"tp": 1 - side},
            device_id_type=MESH,
        )

    def trade_grad(piece):
        return pltpu.make_async_remote_copy(
            src_ref=mine.at[piece],
            dst_ref=grads.at[piece],
            send_sem=g_send.at[piece],
            recv_sem=g_recv.at[piece],
            device_id={"tp": 1 - side},
            device_id_type=MESH,
        )

    def keep_late(piece):
        at = piece - (own_chunks - LATE)
        return pltpu.make_async_copy(mine.at[piece], late_mine.at[at], late_sem.at[at])

    def keep_act(piece):
        return pltpu.make_async_copy(came.at[piece], act.at[piece], act_sem.at[piece])

    def keep_taken(chunk):
        place_at = column(chunk) + chunks * (chunk // chunks)
        return pltpu.make_async_copy(
            taken.at[chunk % 3], both.at[place_at], out_sem.at[chunk % 3]
        )

    def fetch_weight(chunk):
        slot = chunk % 2
        return pltpu.make_async_copy(both.at[column(chunk)], again.at[slot], again_sem.at[slot])

    rate = rates[lr_index[me]]
    decay = 0.9 * rate
    load_tokens = pltpu.make_async_copy(tokens, tok_v, load_sem.at[0])
    load_cot = pltpu.make_async_copy(cot, cot_v, load_sem.at[1])
    keep_turned = pltpu.make_async_copy(turn_v, turned, load_sem.at[2])

    load_own(weight, 0).start()
    load_tokens.start()
    load_own(weight, 1).start()
    load_own(weight, 2).start()
    load_cot.start()
    barrier = pltpu.get_barrier_semaphore()
    for near in (target, origin, partner):
        pl.semaphore_signal(barrier, inc=1, device_id={"pop": near}, device_id_type=MESH)
    pl.semaphore_signal(barrier, inc=1, device_id={"tp": 1 - side}, device_id_type=MESH)
    pl.semaphore_wait(barrier, 4)
    load_own(weight, 0).wait()
    lend(0).start()
    load_tokens.wait()

    def ring_step(chunk, sub, step):
        piece = sub % SPLIT
        cut = pl.ds((sub // SPLIT) * SUB, SUB)

        @pl.when(jnp.logical_and(step >= DEPTH, step < steps))
        def _():
            onward(step - DEPTH).wait_recv()

        @pl.when(jnp.logical_and(chunk < all_chunks, step < DEPTH))
        def _():
            held = own[chunk % slots, half_rows(core, piece), cut]
            lent = other[chunk % LENT, pl.ds(piece * part, part), cut]
            hold[step] = jnp.where(is_root, held, lent)

        @pl.when(jnp.logical_and(chunk < all_chunks, step >= DEPTH))
        def _():
            held = own[chunk % slots, half_rows(core, piece), cut]
            lent = other[chunk % LENT, pl.ds(piece * part, part), cut]
            hold[step] = jnp.where(is_root, held, jnp.where(partner_root, lent, hold[step]))

        @pl.when(step + DEPTH < steps)
        def _():
            @pl.when(step >= THROTTLE)
            def _():
                onward(step - THROTTLE).wait_send()

            onward(step).start()

        @pl.when(step < steps)
        def _():
            @pl.when(step >= THROTTLE)
            def _():
                across(step - THROTTLE).wait_send()

            across(step).start()

        @pl.when(jnp.logical_and(step >= LAG, step < steps + LAG))
        def _():
            across(step - LAG).wait_recv()

    def consume(chunk, sub):
        piece = sub % SPLIT
        cut = pl.ds((sub // SPLIT) * SUB, SUB)
        unit = chunk * per + sub
        for way, source, gap in ((core, hold, own_gap), (1 - core, mirror, mirror_gap)):
            value = source[unit]
            for hop in range(1, chips):
                value = jnp.where(gap == hop, source[unit + hop * DEPTH], value)
            held = own[chunk % slots, half_rows(way, piece), cut]
            taken[chunk % 3, half_rows(way, piece), cut] = jnp.where(chosen, value, held)

    def finish(chunk):
        @pl.when(chunk < chunks)
        def _():
            value = jnp.dot(
                tok_v[...], taken[chunk % 3], preferred_element_type=jnp.float32
            ).astype(jnp.bfloat16)

            @pl.when(chunk < own_chunks)
            def _():
                theirs[chunk] = value

            @pl.when(chunk >= own_chunks)
            def _():
                mine[chunk - own_chunks] = value

        @pl.when(chunk >= chunks)
        def _():
            fetch_weight(chunk).wait()
            slot = chunk % 3
            tall = 128

            def fold(at, extra):
                kept = again[chunk % 2, at, :].astype(jnp.float32)
                moved = taken[slot, at, :].astype(jnp.float32)
                taken[slot, at, :] = (kept - decay * moved - extra).astype(jnp.bfloat16)

            @pl.when(chunk < chunks + own_chunks)
            def _():
                def strip(index, carry):
                    fold(pl.ds(pl.multiple_of(index * tall, tall), tall), 0.0)
                    return carry

                lax.fori_loop(0, rows // tall, strip, 0)

            @pl.when(chunk >= chunks + own_chunks)
            def _():
                for top in (0, half):
                    at = pl.ds(top, half)
                    value = jnp.dot(
                        turn_v[at, :],
                        mine[chunk - chunks - own_chunks],
                        preferred_element_type=jnp.float32,
                    )
                    fold(at, rate * value)

        keep_taken(chunk).start()

    def gradient(piece, sub):
        if sub == 0:
            trade(piece).wait_recv()
        cut = pl.ds(pl.multiple_of(piece * CHUNK, CHUNK), CHUNK)
        tall = 64

        def strip(index, carry):
            at = pl.ds(pl.multiple_of(index * tall, tall), tall)
            value = mine[piece, at, :].astype(jnp.float32) + came[piece, at, :].astype(jnp.float32)
            slope = math.sqrt(2 / math.pi)
            square = value * value
            bent = jnp.tanh(slope * (value + 0.044715 * (square * value)))
            gate = 0.5 * (1.0 + bent)
            rise = 0.5 * value * (1.0 - bent * bent) * (slope * (1.0 + 0.134145 * square))
            came[piece, at, :] = (value * gate).astype(jnp.bfloat16)
            mine[piece, at, :] = (cot_v[at, cut].astype(jnp.float32) * (gate + rise)).astype(
                jnp.bfloat16
            )
            return carry

        strips = tok_v.shape[0] // tall // per
        lax.fori_loop(strips * sub, strips * (sub + 1), strip, 0)
        if sub < per - 1:
            return
        keep_act(piece).start()

        @pl.when(piece >= own_chunks - LATE)
        def _():
            keep_late(piece).start()

    def send_piece(piece):
        @pl.when(piece < own_chunks)
        def _():
            trade(piece).start()

        @pl.when(piece >= own_chunks)
        def _():
            trade_grad(piece - own_chunks).start()

    def sent_piece(piece):
        @pl.when(piece < own_chunks)
        def _():
            trade(piece).wait_send()

        @pl.when(piece >= own_chunks)
        def _():
            trade_grad(piece - own_chunks).wait_send()

    def issue(piece):
        @pl.when(piece >= FLYING)
        def _():
            sent_piece(piece - FLYING)

        send_piece(piece)

    pace_from = behind + per
    pieces = 2 * own_chunks - LATE
    in_loop = min(pieces, 2 * (rounds * per - 1 - pace_from) // PACE + 1)

    def turn(chunk, carry):
        @pl.when(chunk < all_chunks)
        def _():
            @pl.when(chunk >= LENT - 1)
            def _():
                lend(chunk - LENT + 1).wait_send()

            @pl.when(chunk + 1 < all_chunks)
            def _():
                load_own(weight, chunk + 1).wait()
                lend(chunk + 1).start()

            @pl.when(chunk + 3 < all_chunks)
            def _():
                start_own(chunk + 3)

            lend(chunk).wait_recv()

        for sub in range(per):
            ring_step(chunk, sub, chunk * per + sub)

            late = chunk + (sub - behind) // per

            if sub == shift:

                @pl.when(jnp.logical_and(late >= 3, late < all_chunks))
                def _():
                    keep_taken(late - 3).wait()

                @pl.when(jnp.logical_and(late >= chunks, late < all_chunks))
                def _():
                    fetch_weight(late).start()

            @pl.when(jnp.logical_and(late >= 0, late < all_chunks))
            def _():
                consume(late, (sub - behind) % per)

            if sub == shift:

                @pl.when(jnp.logical_and(late >= 1, late <= all_chunks))
                def _():
                    finish(late - 1)
            else:
                turns = [other_sub for other_sub in range(per) if other_sub != shift]
                since = chunk - GRAD_FIRST
                if sub == turns[0]:
                    quarters = range(per - len(turns) + 1)
                else:
                    quarters = (per - len(turns) + turns.index(sub),)

                @pl.when(
                    jnp.logical_and(
                        since >= 0,
                        jnp.logical_and(
                            since % GRAD_EVERY == 0, since // GRAD_EVERY < own_chunks
                        ),
                    )
                )
                def _():
                    for quarter in quarters:
                        gradient(since // GRAD_EVERY, quarter)

            paced = chunk * per + sub - pace_from

            @pl.when(
                jnp.logical_and(
                    paced >= 0,
                    jnp.logical_and(2 * paced % PACE < 2, 2 * paced // PACE < in_loop),
                )
            )
            def _():
                issue(2 * paced // PACE)

        @pl.when(chunk == 2)
        def _():
            turn_v[...] = tok_v[...].T
            keep_turned.start()

        @pl.when(chunk == GRAD_FIRST - 1)
        def _():
            load_cot.wait()

        return carry

    lax.fori_loop(0, rounds, turn, 0)

    for step in range(steps - DEPTH - THROTTLE, steps - DEPTH):
        onward(step).wait_send()
    for step in range(steps - THROTTLE, steps):
        across(step).wait_send()
    for chunk in range(all_chunks - LENT + 1, all_chunks):
        lend(chunk).wait_send()
    for chunk in range(all_chunks - 3, all_chunks):
        keep_taken(chunk).wait()
    keep_turned.wait()

    def rest(piece, carry):
        issue(piece)
        return carry

    lax.fori_loop(in_loop, pieces, rest, 0)
    for piece in range(pieces - FLYING, pieces):
        sent_piece(piece)

    def drain(piece, carry):
        keep_act(piece).wait()

        @pl.when(piece < own_chunks - LATE)
        def _():
            trade_grad(piece).wait_recv()

        @pl.when(piece >= own_chunks - LATE)
        def _():
            keep_late(piece).wait()

        return carry

    lax.fori_loop(0, own_chunks, drain, 0)


def fused(assignment, lr_index, rates, tokens, weight, momentum, cot, members):
    rows, cols = weight.shape
    count, share = cot.shape
    chunks = cols // CHUNK
    own_chunks = chunks // 2
    per = SPLIT * (CHUNK // SUB)
    chips = members // 2
    fill = (chips - 1) * DEPTH
    steps = 2 * chunks * per + fill
    slots = (fill + LAG + per - 1) // per + 4
    part = rows // 2 // SPLIT
    kind = weight.dtype
    dma = pltpu.SemaphoreType.DMA
    anywhere = pl.BlockSpec(memory_space=pl.ANY)
    return pl.pallas_call(
        functools.partial(fused_kernel, members),
        out_shape=(
            jax.ShapeDtypeStruct((2 * chunks, rows, CHUNK), kind),
            jax.ShapeDtypeStruct((own_chunks - LATE, count, CHUNK), kind),
            jax.ShapeDtypeStruct((own_chunks, count, CHUNK), kind),
            jax.ShapeDtypeStruct((rows, count), kind),
            jax.ShapeDtypeStruct((LATE, count, CHUNK), kind),
        ),
        in_specs=[pl.BlockSpec(memory_space=pltpu.SMEM)] * 3 + [anywhere] * 4,
        out_specs=(anywhere,) * 5,
        scratch_shapes=[
            pltpu.VMEM((steps, part, SUB), kind),
            pltpu.VMEM((steps, part, SUB), kind),
            pltpu.VMEM((slots, rows, CHUNK), kind),
            pltpu.VMEM((LENT, rows // 2, CHUNK), kind),
            pltpu.VMEM((3, rows, CHUNK), kind),
            pltpu.VMEM((own_chunks, count, CHUNK), kind),
            pltpu.VMEM((own_chunks, count, CHUNK), kind),
            pltpu.VMEM((own_chunks, count, CHUNK), kind),
            pltpu.VMEM((2, rows, CHUNK), kind),
            pltpu.VMEM((count, share), kind),
            pltpu.VMEM((count, rows), kind),
            pltpu.VMEM((rows, count), kind),
            dma((slots,)),
            dma((LENT,)),
            dma((2 * chunks,)),
            dma((THROTTLE,)),
            dma((steps,)),
            dma((THROTTLE,)),
            dma((steps,)),
            dma((own_chunks,)),
            dma((own_chunks,)),
            dma((own_chunks,)),
            dma((own_chunks,)),
            dma((3,)),
            dma((own_chunks,)),
            dma((LATE,)),
            dma((2,)),
            dma((3,)),
        ],
        compiler_params=pltpu.CompilerParams(
            collective_id=0, has_side_effects=True, vmem_limit_bytes=60 * 2**20
        ),
        name="fused",
    )(assignment, lr_index, rates, tokens, weight, momentum, cot)


def settle_kernel(first, lr_index, rates, turned, both, grads, extra, out, *rest):
    *active, turn_v, base_v, grad_v, turn_sem, base_sem, grad_sem, out_sem = rest[: len(rest) - 4 * (len(rest) > 8)]
    rows = turned.shape[0]
    chunks = both.shape[0] // 2
    own_chunks = chunks // 2
    count = grad_v.shape[0]
    side = lax.axis_index("tp")
    rate = rates[lr_index[lax.axis_index("pop")]]
    if active:
        copy_v, act_v, copy_sem, act_sem = rest[-4:]

    def each(total, act):
        def body(index, carry):
            act(index)
            return carry

        lax.fori_loop(0, total, body, 0)

    def cut(at):
        return pl.ds(pl.multiple_of(at * CHUNK, CHUNK), CHUNK)

    def far(step):
        return (1 - side) * own_chunks + first + step

    def near(step):
        return side * own_chunks + step

    def load_base(step):
        return pltpu.make_async_copy(
            both.at[chunks + far(step)], base_v.at[step], base_sem.at[step]
        )

    def load_grad(step):
        return pltpu.make_async_copy(grads.at[step], grad_v.at[step], grad_sem.at[step])

    def store(step):
        return pltpu.make_async_copy(base_v.at[step], out.at[:, cut(far(step))], out_sem.at[step])

    def load_copy(step):
        return pltpu.make_async_copy(
            both.at[chunks + near(step)], copy_v.at[step], copy_sem.at[0, step]
        )

    def store_copy(step):
        return pltpu.make_async_copy(
            copy_v.at[step], out.at[:, cut(near(step))], copy_sem.at[1, step]
        )

    def load_act(step):
        return pltpu.make_async_copy(extra.at[step], act_v.at[step], act_sem.at[0, step])

    def store_act(step):
        return pltpu.make_async_copy(
            act_v.at[step], active[0].at[:, cut(step)], act_sem.at[1, step]
        )

    load_turned = pltpu.make_async_copy(turned, turn_v, turn_sem.at[0])
    load_turned.start()

    def begin(step):
        load_base(step).start()
        load_grad(step).start()

    def begin_copy(step):
        load_copy(step).start()
        load_act(step).start()

    each(count, begin)
    if active:
        each(own_chunks, begin_copy)
    load_turned.wait()

    def work(step):
        load_base(step).wait()
        load_grad(step).wait()
        for top in (0, rows // 2):
            at = pl.ds(top, rows // 2)
            grad_weight = jnp.dot(
                turn_v[at, :], grad_v[step], preferred_element_type=jnp.float32
            )
            base = base_v[step, at, :].astype(jnp.float32)
            base_v[step, at, :] = (base - rate * grad_weight).astype(base_v.dtype)
        store(step).start()

    each(count, work)
    if active:

        def hand_on(step):
            load_copy(step).wait()
            store_copy(step).start()
            load_act(step).wait()
            store_act(step).start()

        each(own_chunks, hand_on)
        each(own_chunks, lambda step: store_copy(step).wait())
        each(own_chunks, lambda step: store_act(step).wait())
    each(count, lambda step: store(step).wait())


def settle(first, count, lr_index, rates, turned, both, grads, extra, last):
    rows, tall = turned.shape
    chunks = both.shape[0] // 2
    own_chunks = chunks // 2
    kind = both.dtype
    scalar = pl.BlockSpec(memory_space=pltpu.SMEM)
    anywhere = pl.BlockSpec(memory_space=pl.ANY)
    dma = pltpu.SemaphoreType.DMA
    whole = jax.ShapeDtypeStruct((rows, chunks * CHUNK), kind)
    scratch = [
        pltpu.VMEM((rows, tall), kind),
        pltpu.VMEM((count, rows, CHUNK), kind),
        pltpu.VMEM((count, tall, CHUNK), kind),
        dma((1,)),
        dma((count,)),
        dma((count,)),
        dma((count,)),
    ]
    if not last:
        scratch += [
            pltpu.VMEM((own_chunks, rows, CHUNK), kind),
            pltpu.VMEM((own_chunks, tall, CHUNK), kind),
            dma((2, own_chunks)),
            dma((2, own_chunks)),
        ]
    return pl.pallas_call(
        functools.partial(settle_kernel, first),
        in_specs=[scalar, scalar] + [anywhere] * 4,
        out_specs=anywhere if last else (anywhere, anywhere),
        out_shape=whole
        if last
        else (whole, jax.ShapeDtypeStruct((tall, own_chunks * CHUNK), kind)),
        scratch_shapes=scratch,
        input_output_aliases={5: 0} if last else {},
        compiler_params=pltpu.CompilerParams(
            vmem_limit_bytes=(LATE_LIMIT if last else 60) * 2**20
        ),
        cost_estimate=pl.CostEstimate(
            flops=2 * rows * tall * count * CHUNK,
            bytes_accessed=6 * rows * count * CHUNK,
            transcendentals=0,
        ),
        name="settle_late" if last else "settle",
    )(lr_index, rates, turned, both, grads, extra)


def local(tokens, weight, momentum, cotangent, assignment, lr_index, rates):
    members = lax.axis_size("pop")
    ranks = lax.axis_size("tp")
    me = lax.axis_index("pop")
    side = lax.axis_index("tp")
    if ranks == 2 and assignment.shape[0] // 4 == 1:
        both, grads, act, turned, late_mine = fused(
            assignment.T, lr_index, rates, tokens[0], weight[0], momentum[0], cotangent[0], members
        )
        late_theirs = lax.ppermute(late_mine, "tp", [(0, 1), (1, 0)])
        count = grads.shape[0]
        partly, active = settle(0, count, lr_index, rates, turned, both, grads, act, False)
        late_theirs, partly = lax.optimization_barrier((late_theirs, partly))
        updated = settle(
            count, LATE, lr_index, rates, turned, both, late_theirs, partly, True
        )
        return (active[None], updated[None])
    member_ids = jnp.arange(members, dtype=jnp.int32)
    hit = assignment[:, 0] == me
    my_source = jnp.where(jnp.any(hit), jnp.sum(jnp.where(hit, assignment[:, 1], 0)), me)
    my_index = jnp.sum(jnp.where(member_ids == me, lr_index, 0))
    rate_ids = jnp.arange(rates.shape[0], dtype=jnp.int32)
    my_rate = jnp.sum(jnp.where(rate_ids == my_index, rates, 0.0))
    tops = assignment.shape[0] // 4
    winner_hit = assignment[:, 1][None, :] == member_ids[:, None]
    present = jnp.any(winner_hit, axis=1)
    roots = jnp.sort(jnp.where(present, member_ids, members))[:tops]
    place = ring_of(me, members)
    tables = []
    for turn in range(tops):
        root = roots[turn]
        chips = members // 2
        root_place = ring_of(root, members)
        behind = (place // 2 - root_place // 2 + chips) % chips
        entries = (
            me == root,
            jnp.logical_and(my_source == root, me != root),
            (behind + chips - 1) % chips,
            (2 * chips - behind - 1) % chips,
            jnp.logical_and(place // 2 == root_place // 2, me != root),
        )
        tables.append(jnp.stack([entry.astype(jnp.int32) for entry in entries]))

    def take(value, first, part=0, parts=1):
        taken = None
        for turn in range(tops):
            arrived = spread(value, tables[turn], members, first + turn, part, parts)
            if taken is None:
                taken = arrived
            else:
                taken = jnp.where(my_source == roots[turn], arrived, taken)
        return taken

    inputs = tokens[0]
    share_cols = cotangent.shape[2]
    taken_weight = take(weight[0], 0)
    partial_value = jnp.dot(inputs, taken_weight, preferred_element_type=jnp.float32)
    partial_value = partial_value.astype(jnp.bfloat16)
    if ranks == 2:
        swap = [(0, 1), (1, 0)]
        left, right = partial_value[:, :share_cols], partial_value[:, share_cols:]
        mine = jnp.where(side == 0, left, right)
        theirs = jnp.where(side == 0, right, left)
        theirs, raw_momentum = lax.optimization_barrier((theirs, momentum[0]))
        arrived = lax.ppermute(theirs, "tp", swap)
        first = take(raw_momentum, tops, 0, 2)
        arrived, first = lax.optimization_barrier((arrived, first))
        hidden = mine.astype(jnp.float32) + arrived.astype(jnp.float32)
        active, grad_mine = activate(hidden, cotangent[0])
        grad_mine, raw_momentum = lax.optimization_barrier((grad_mine, raw_momentum))
        grad_theirs = lax.ppermute(grad_mine, "tp", swap)
        second = take(raw_momentum, 2 * tops, 1, 2)
        updated = update(
            side.astype(jnp.int32).reshape(1),
            my_rate.reshape(1),
            inputs.T,
            grad_mine,
            grad_theirs,
            taken_weight,
            first,
            second,
        )
    else:
        taken_momentum = take(momentum[0], tops)
        hidden = lax.psum_scatter(
            partial_value, "tp", scatter_dimension=1, tiled=True
        ).astype(jnp.float32)
        active, grad_mine = activate(hidden, cotangent[0])
        grad_hidden = lax.all_gather(grad_mine, "tp", axis=1, tiled=True)
        grad_weight = lax.dot_general(
            inputs, grad_hidden, (((0,), (0,)), ((), ())), preferred_element_type=jnp.float32
        )
        new_momentum = 0.9 * taken_momentum.astype(jnp.float32) + grad_weight
        updated = taken_weight.astype(jnp.float32) - my_rate * new_momentum
        updated = updated.astype(jnp.bfloat16)
    return (active[None], updated[None])


def solution(mesh):
    placed = (
        P("pop", None, "tp"),
        P("pop", "tp", None),
        P("pop", "tp", None),
        P("pop", None, "tp"),
        P(),
        P(),
        P(),
    )
    return jax.shard_map(
        local,
        mesh=mesh,
        in_specs=placed,
        out_specs=(P("pop", None, "tp"), P("pop", "tp", None)),
        check_vma=False,
    )
```

```python
import functools
import math

import jax
import jax.numpy as jnp
from jax import lax
from jax.experimental import pallas as pl
from jax.experimental.pallas import tpu as pltpu
from jax.sharding import PartitionSpec as P

MESH = pl.DeviceIdType.MESH
PIECES = 4
TILE = 512


def ring_of(member, members):
    core = member % 2
    y = (member // 2) % 2
    z = member // 4
    half = members // 4
    chip = z * (1 - y) + (2 * half - 1 - z) * y
    return 2 * chip + core


def member_at(place, members):
    core = place % 2
    chip = place // 2
    half = members // 4
    y = chip // half
    z = chip * (1 - y) + (2 * half - 1 - chip) * y
    return (2 * z + y) * 2 + core


def gelu_tanh(value):
    return jax.nn.gelu(value, approximate=True)


def activate(hidden, cot_block):
    active, pullback = jax.vjp(gelu_tanh, hidden)
    grad_hidden = pullback(cot_block.astype(jnp.float32))[0].astype(jnp.bfloat16)
    return (active.astype(jnp.bfloat16), grad_hidden)


def rows_of(rows, cols, whole_cols):
    wanted = 16 * (whole_cols // cols)
    return wanted if (rows // 2) % wanted == 0 else 16


def spread_kernel(
    members, height, table, own, out, came, mirror, other, sent,
    send_sem, recv_sem, near_send, near_recv, back_send, back_recv,
):
    rows, cols = own.shape
    half = rows // 2
    blocks = half // height
    chips = members // 2
    steps = blocks + chips - 1
    width = cols // PIECES
    place = ring_of(lax.axis_index("pop"), members)
    chip = place // 2
    core = place % 2
    target = member_at(2 * ((chip + 1 - 2 * core + chips) % chips) + core, members)
    origin = member_at(2 * ((chip - 1 + 2 * core + chips) % chips) + core, members)
    partner = member_at(2 * chip + 1 - core, members)
    is_root = table[0] > 0
    chosen = table[1] > 0
    partner_root = table[4] > 0

    barrier = pltpu.get_barrier_semaphore()
    for near in (target, origin, partner):
        pl.semaphore_signal(barrier, inc=1, device_id={"pop": near}, device_id_type=MESH)
    pl.semaphore_wait(barrier, 3)

    def block_rows(way, block):
        return pl.ds(pl.multiple_of(way * half + block * height, height), height)

    def lend(block):
        return pltpu.make_async_remote_copy(
            src_ref=own.at[block_rows(1 - core, block), :],
            dst_ref=other.at[block],
            send_sem=near_send.at[block],
            recv_sem=near_recv.at[block],
            device_id={"pop": partner},
            device_id_type=MESH,
        )

    def onward(step, piece):
        cut = pl.ds(piece * width, width)
        return pltpu.make_async_remote_copy(
            src_ref=sent.at[step % 2, :, cut],
            dst_ref=came.at[step, :, cut],
            send_sem=send_sem.at[step % 2, piece],
            recv_sem=recv_sem.at[step, piece],
            device_id={"pop": target},
            device_id_type=MESH,
        )

    def across(step):
        return pltpu.make_async_remote_copy(
            src_ref=came.at[step],
            dst_ref=mirror.at[step],
            send_sem=back_send.at[step],
            recv_sem=back_recv.at[step],
            device_id={"pop": partner},
            device_id_type=MESH,
        )

    def each(count, act):
        def body(index, carry):
            act(index)
            return carry

        lax.fori_loop(0, count, body, 0)

    each(blocks, lambda block: lend(block).start())
    lend(0).wait_recv()
    for piece in range(PIECES):
        cut = pl.ds(piece * width, width)
        sent[0, :, cut] = jnp.where(is_root, own[block_rows(core, 0), cut], other[0, :, cut])
        onward(0, piece).start()

    def forward(step, carry):
        block = jnp.minimum(step, blocks - 1)

        @pl.when(step < blocks)
        def _():
            lend(step).wait_recv()

        for piece in range(PIECES):
            cut = pl.ds(piece * width, width)
            onward(step - 1, piece).wait_recv()

            @pl.when(step >= 2)
            def _():
                onward(step - 2, piece).wait_send()

            relayed = jnp.where(partner_root, other[block, :, cut], came[step - 1, :, cut])
            sent[step % 2, :, cut] = jnp.where(
                is_root, own[block_rows(core, block), cut], relayed
            )
            onward(step, piece).start()
        across(step - 1).start()
        return carry

    lax.fori_loop(1, steps, forward, 0)
    for piece in range(PIECES):
        onward(steps - 1, piece).wait_recv()
    across(steps - 1).start()

    def settle(block):
        at = block_rows(core, block)
        out[at, :] = jnp.where(chosen, came[block + table[2 + core]], own[at, :])

    each(blocks, settle)
    each(steps, lambda step: across(step).wait_recv())

    def settle_other(block):
        at = block_rows(1 - core, block)
        out[at, :] = jnp.where(chosen, mirror[block + table[3 - core]], own[at, :])

    each(blocks, settle_other)
    for piece in range(PIECES):
        onward(steps - 2, piece).wait_send()
        onward(steps - 1, piece).wait_send()
    each(blocks, lambda block: lend(block).wait_send())
    each(steps, lambda step: across(step).wait_send())


def spread(value, table, members, turn, part, parts):
    rows, whole_cols = value.shape
    cols = whole_cols // parts
    height = rows_of(rows, cols, whole_cols)
    blocks = rows // 2 // height
    steps = blocks + members // 2 - 1
    return pl.pallas_call(
        functools.partial(spread_kernel, members, height),
        grid=(1,),
        out_shape=jax.ShapeDtypeStruct((rows, cols), value.dtype),
        in_specs=[
            pl.BlockSpec(memory_space=pltpu.SMEM),
            pl.BlockSpec((rows, cols), lambda i: (0, part), pipeline_mode=pl.Buffered(1)),
        ],
        out_specs=pl.BlockSpec((rows, cols), lambda i: (0, 0), pipeline_mode=pl.Buffered(1)),
        scratch_shapes=[
            pltpu.VMEM((steps, height, cols), value.dtype),
            pltpu.VMEM((steps, height, cols), value.dtype),
            pltpu.VMEM((blocks, height, cols), value.dtype),
            pltpu.VMEM((2, height, cols), value.dtype),
            pltpu.SemaphoreType.DMA((2, PIECES)),
            pltpu.SemaphoreType.DMA((steps, PIECES)),
            pltpu.SemaphoreType.DMA((blocks,)),
            pltpu.SemaphoreType.DMA((blocks,)),
            pltpu.SemaphoreType.DMA((steps,)),
            pltpu.SemaphoreType.DMA((steps,)),
        ],
        compiler_params=pltpu.CompilerParams(
            collective_id=turn, has_side_effects=True, vmem_limit_bytes=60 * 2**20
        ),
        cost_estimate=pl.CostEstimate(
            flops=0, bytes_accessed=300 * 2**20 // parts, transcendentals=0
        ),
        name=f"spread_{turn}",
    )(table, value)


def update_kernel(half, side, rate, turned, mine, theirs, weight, first, second, out):
    block = pl.program_id(0)
    grad = jnp.where(block // half == side[0], mine[...], theirs[...])
    grad_weight = jnp.dot(turned[...], grad, preferred_element_type=jnp.float32)
    momentum = jnp.where(block < half, first[...], second[...]).astype(jnp.float32)
    new_momentum = 0.9 * momentum + grad_weight
    out[...] = (weight[...].astype(jnp.float32) - rate[0] * new_momentum).astype(out.dtype)


def update(side, rate, turned, mine, theirs, weight, first, second):
    rows, cols = weight.shape
    tokens = turned.shape[1]
    half = cols // 2 // TILE
    near = lambda j, side: (0, jnp.clip(j - side[0] * half, 0, half - 1))
    far = lambda j, side: (0, jnp.clip(j - (1 - side[0]) * half, 0, half - 1))
    return pl.pallas_call(
        functools.partial(update_kernel, half),
        grid_spec=pltpu.PrefetchScalarGridSpec(
            num_scalar_prefetch=1,
            grid=(2 * half,),
            in_specs=[
                pl.BlockSpec(memory_space=pltpu.SMEM),
                pl.BlockSpec((rows, tokens), lambda j, side: (0, 0)),
                pl.BlockSpec((tokens, TILE), near),
                pl.BlockSpec((tokens, TILE), far),
                pl.BlockSpec((rows, TILE), lambda j, side: (0, j)),
                pl.BlockSpec((rows, TILE), lambda j, side: (0, jnp.minimum(j, half - 1))),
                pl.BlockSpec((rows, TILE), lambda j, side: (0, jnp.maximum(j - half, 0))),
            ],
            out_specs=pl.BlockSpec((rows, TILE), lambda j, side: (0, j)),
        ),
        out_shape=jax.ShapeDtypeStruct(weight.shape, weight.dtype),
        compiler_params=pltpu.CompilerParams(vmem_limit_bytes=40 * 2**20),
        cost_estimate=pl.CostEstimate(
            flops=2 * rows * cols * tokens,
            bytes_accessed=6 * rows * cols,
            transcendentals=0,
        ),
        name="update",
    )(side, rate, turned, mine, theirs, weight, first, second)


SUB = 128
CHUNK = 256
SPLIT = 2
DEPTH = 5
LAG = 5
LENT = 4
THROTTLE = 8
GRAD_FIRST = 30
FLYING = 3
PACE = 17
LATE = 3
LATE_LIMIT = 60
GRAD_EVERY = 2


def fused_kernel(
    members, assign, lr_index, rates, tokens, weight, momentum, cot,
    both, grads, act, turned, late_mine,
    hold, mirror, own, other, taken, theirs, came, mine, again, cot_v, tok_v, turn_v,
    own_sem, lend_send, lend_recv, ring_send, ring_recv, back_send, back_recv,
    x_send, x_recv, g_send, g_recv, out_sem, act_sem, late_sem, again_sem, load_sem,
):
    rows, cols = weight.shape
    half = rows // 2
    part = half // SPLIT
    chunks = cols // CHUNK
    own_chunks = chunks // 2
    per = SPLIT * (CHUNK // SUB)
    all_chunks = 2 * chunks
    units = all_chunks * per
    chips = members // 2
    fill = (chips - 1) * DEPTH
    steps = units + fill + fill % 2
    behind = fill + LAG
    shift = behind % per
    rounds = all_chunks + (behind + per - 1) // per + 1
    slots = own.shape[0]

    me = lax.axis_index("pop")
    side = lax.axis_index("tp")
    place = ring_of(me, members)
    chip = place // 2
    core = place % 2
    target = member_at(2 * ((chip + 1 - 2 * core + chips) % chips) + core, members)
    origin = member_at(2 * ((chip - 1 + 2 * core + chips) % chips) + core, members)
    partner = member_at(2 * chip + 1 - core, members)

    root = assign[1, 0]
    root_chip = ring_of(root, members) // 2
    is_root = me == root
    partner_root = partner == root
    chosen = assign[0, 0] == me
    for row in range(1, assign.shape[1]):
        chosen = jnp.logical_or(chosen, assign[0, row] == me)
    forward_gap = (chip - root_chip + chips) % chips
    backward_gap = (root_chip - chip + chips) % chips
    own_gap = jnp.where(core == 0, forward_gap, backward_gap)
    mirror_gap = jnp.where(core == 0, backward_gap, forward_gap)

    def column(chunk):
        at = chunk % chunks
        first = at < own_chunks
        return jnp.where(first, (1 - side) * own_chunks + at, side * own_chunks + at - own_chunks)

    def half_rows(way, piece):
        return pl.ds(pl.multiple_of(way * half + piece * part, 16), part)

    def load_own(source, chunk):
        cut = pl.ds(pl.multiple_of(column(chunk) * CHUNK, CHUNK), CHUNK)
        slot = chunk % slots
        return pltpu.make_async_copy(source.at[:, cut], own.at[slot], own_sem.at[slot])

    def start_own(chunk):
        @pl.when(chunk < chunks)
        def _():
            load_own(weight, chunk).start()

        @pl.when(chunk >= chunks)
        def _():
            load_own(momentum, chunk).start()

    def lend(chunk):
        away = pl.ds(pl.multiple_of((1 - core) * half, 16), half)
        return pltpu.make_async_remote_copy(
            src_ref=own.at[chunk % slots, away, :],
            dst_ref=other.at[chunk % LENT],
            send_sem=lend_send.at[chunk % LENT],
            recv_sem=lend_recv.at[chunk],
            device_id={"pop": partner},
            device_id_type=MESH,
        )

    def onward(step):
        return pltpu.make_async_remote_copy(
            src_ref=hold.at[step],
            dst_ref=hold.at[step + DEPTH],
            send_sem=ring_send.at[step % THROTTLE],
            recv_sem=ring_recv.at[step + DEPTH],
            device_id={"pop": target},
            device_id_type=MESH,
        )

    def across(pair):
        both_steps = pl.ds(2 * pair, 2)
        return pltpu.make_async_remote_copy(
            src_ref=hold.at[both_steps],
            dst_ref=mirror.at[both_steps],
            send_sem=back_send.at[pair % THROTTLE],
            recv_sem=back_recv.at[pair],
            device_id={"pop": partner},
            device_id_type=MESH,
        )

    def trade(piece):
        return pltpu.make_async_remote_copy(
            src_ref=theirs.at[piece],
            dst_ref=came.at[piece],
            send_sem=x_send.at[piece],
            recv_sem=x_recv.at[piece],
            device_id={"tp": 1 - side},
            device_id_type=MESH,
        )

    def trade_grad(piece):
        return pltpu.make_async_remote_copy(
            src_ref=mine.at[piece],
            dst_ref=grads.at[piece],
            send_sem=g_send.at[piece],
            recv_sem=g_recv.at[piece],
            device_id={"tp": 1 - side},
            device_id_type=MESH,
        )

    def keep_late(piece):
        at = piece - (own_chunks - LATE)
        return pltpu.make_async_copy(mine.at[piece], late_mine.at[at], late_sem.at[at])

    def keep_act(piece):
        return pltpu.make_async_copy(came.at[piece], act.at[piece], act_sem.at[piece])

    def keep_taken(chunk):
        place_at = column(chunk) + chunks * (chunk // chunks)
        return pltpu.make_async_copy(
            taken.at[chunk % 3], both.at[place_at], out_sem.at[chunk % 3]
        )

    def fetch_weight(chunk):
        slot = chunk % 2
        return pltpu.make_async_copy(both.at[column(chunk)], again.at[slot], again_sem.at[slot])

    rate = rates[lr_index[me]]
    decay = 0.9 * rate
    load_tokens = pltpu.make_async_copy(tokens, tok_v, load_sem.at[0])
    load_cot = pltpu.make_async_copy(cot, cot_v, load_sem.at[1])
    keep_turned = pltpu.make_async_copy(turn_v, turned, load_sem.at[2])

    load_own(weight, 0).start()
    load_tokens.start()
    load_own(weight, 1).start()
    load_own(weight, 2).start()
    load_cot.start()
    barrier = pltpu.get_barrier_semaphore()
    for near in (target, origin, partner):
        pl.semaphore_signal(barrier, inc=1, device_id={"pop": near}, device_id_type=MESH)
    pl.semaphore_signal(barrier, inc=1, device_id={"tp": 1 - side}, device_id_type=MESH)
    pl.semaphore_wait(barrier, 4)
    load_own(weight, 0).wait()
    lend(0).start()
    load_tokens.wait()

    def ring_step(chunk, sub, step):
        piece = sub % SPLIT
        cut = pl.ds((sub // SPLIT) * SUB, SUB)

        @pl.when(jnp.logical_and(step >= DEPTH, step < steps))
        def _():
            onward(step - DEPTH).wait_recv()

        @pl.when(jnp.logical_and(chunk < all_chunks, step < DEPTH))
        def _():
            held = own[chunk % slots, half_rows(core, piece), cut]
            lent = other[chunk % LENT, pl.ds(piece * part, part), cut]
            hold[step] = jnp.where(is_root, held, lent)

        @pl.when(jnp.logical_and(chunk < all_chunks, step >= DEPTH))
        def _():
            held = own[chunk % slots, half_rows(core, piece), cut]
            lent = other[chunk % LENT, pl.ds(piece * part, part), cut]
            hold[step] = jnp.where(is_root, held, jnp.where(partner_root, lent, hold[step]))

        @pl.when(step + DEPTH < steps)
        def _():
            @pl.when(step >= THROTTLE)
            def _():
                onward(step - THROTTLE).wait_send()

            onward(step).start()

        if sub % 2 == 1:
            pair = step // 2

            @pl.when(step < steps)
            def _():
                @pl.when(pair >= THROTTLE)
                def _():
                    across(pair - THROTTLE).wait_send()

                across(pair).start()

        if (sub - LAG) % 2 == 0:

            @pl.when(jnp.logical_and(step >= LAG, step < steps + LAG))
            def _():
                across((step - LAG) // 2).wait_recv()

    def consume(chunk, sub):
        piece = sub % SPLIT
        cut = pl.ds((sub // SPLIT) * SUB, SUB)
        unit = chunk * per + sub
        for way, source, gap in ((core, hold, own_gap), (1 - core, mirror, mirror_gap)):
            value = source[unit]
            for hop in range(1, chips):
                value = jnp.where(gap == hop, source[unit + hop * DEPTH], value)
            held = own[chunk % slots, half_rows(way, piece), cut]
            taken[chunk % 3, half_rows(way, piece), cut] = jnp.where(chosen, value, held)

    def finish(chunk):
        @pl.when(chunk < chunks)
        def _():
            value = jnp.dot(
                tok_v[...], taken[chunk % 3], preferred_element_type=jnp.float32
            ).astype(jnp.bfloat16)

            @pl.when(chunk < own_chunks)
            def _():
                theirs[chunk] = value

            @pl.when(chunk >= own_chunks)
            def _():
                mine[chunk - own_chunks] = value

        @pl.when(chunk >= chunks)
        def _():
            fetch_weight(chunk).wait()
            slot = chunk % 3
            tall = 128

            def fold(at, extra):
                kept = again[chunk % 2, at, :].astype(jnp.float32)
                moved = taken[slot, at, :].astype(jnp.float32)
                taken[slot, at, :] = (kept - decay * moved - extra).astype(jnp.bfloat16)

            @pl.when(chunk < chunks + own_chunks)
            def _():
                def strip(index, carry):
                    fold(pl.ds(pl.multiple_of(index * tall, tall), tall), 0.0)
                    return carry

                lax.fori_loop(0, rows // tall, strip, 0)

            @pl.when(chunk >= chunks + own_chunks)
            def _():
                for top in (0, half):
                    at = pl.ds(top, half)
                    value = jnp.dot(
                        turn_v[at, :],
                        mine[chunk - chunks - own_chunks],
                        preferred_element_type=jnp.float32,
                    )
                    fold(at, rate * value)

        keep_taken(chunk).start()

    def gradient(piece, sub):
        if sub == 0:
            trade(piece).wait_recv()
        cut = pl.ds(pl.multiple_of(piece * CHUNK, CHUNK), CHUNK)
        tall = 64

        def strip(index, carry):
            at = pl.ds(pl.multiple_of(index * tall, tall), tall)
            value = mine[piece, at, :].astype(jnp.float32) + came[piece, at, :].astype(jnp.float32)
            slope = math.sqrt(2 / math.pi)
            square = value * value
            bent = jnp.tanh(slope * (value + 0.044715 * (square * value)))
            gate = 0.5 * (1.0 + bent)
            rise = 0.5 * value * (1.0 - bent * bent) * (slope * (1.0 + 0.134145 * square))
            came[piece, at, :] = (value * gate).astype(jnp.bfloat16)
            mine[piece, at, :] = (cot_v[at, cut].astype(jnp.float32) * (gate + rise)).astype(
                jnp.bfloat16
            )
            return carry

        strips = tok_v.shape[0] // tall // per
        lax.fori_loop(strips * sub, strips * (sub + 1), strip, 0)
        if sub < per - 1:
            return
        keep_act(piece).start()

        @pl.when(piece >= own_chunks - LATE)
        def _():
            keep_late(piece).start()

    def send_piece(piece):
        @pl.when(piece < own_chunks)
        def _():
            trade(piece).start()

        @pl.when(piece >= own_chunks)
        def _():
            trade_grad(piece - own_chunks).start()

    def sent_piece(piece):
        @pl.when(piece < own_chunks)
        def _():
            trade(piece).wait_send()

        @pl.when(piece >= own_chunks)
        def _():
            trade_grad(piece - own_chunks).wait_send()

    def issue(piece):
        @pl.when(piece >= FLYING)
        def _():
            sent_piece(piece - FLYING)

        send_piece(piece)

    pace_from = behind + per
    pieces = 2 * own_chunks - LATE
    in_loop = min(pieces, 2 * (rounds * per - 1 - pace_from) // PACE + 1)

    def turn(chunk, carry):
        @pl.when(chunk < all_chunks)
        def _():
            @pl.when(chunk >= LENT - 1)
            def _():
                lend(chunk - LENT + 1).wait_send()

            @pl.when(chunk + 1 < all_chunks)
            def _():
                load_own(weight, chunk + 1).wait()
                lend(chunk + 1).start()

            @pl.when(chunk + 3 < all_chunks)
            def _():
                start_own(chunk + 3)

            lend(chunk).wait_recv()

        for sub in range(per):
            ring_step(chunk, sub, chunk * per + sub)

            late = chunk + (sub - behind) // per

            if sub == shift:

                @pl.when(jnp.logical_and(late >= 3, late < all_chunks))
                def _():
                    keep_taken(late - 3).wait()

                @pl.when(jnp.logical_and(late >= chunks, late < all_chunks))
                def _():
                    fetch_weight(late).start()

            @pl.when(jnp.logical_and(late >= 0, late < all_chunks))
            def _():
                consume(late, (sub - behind) % per)

            if sub == shift:

                @pl.when(jnp.logical_and(late >= 1, late <= all_chunks))
                def _():
                    finish(late - 1)
            else:
                turns = [other_sub for other_sub in range(per) if other_sub != shift]
                since = chunk - GRAD_FIRST
                if sub == turns[0]:
                    quarters = range(per - len(turns) + 1)
                else:
                    quarters = (per - len(turns) + turns.index(sub),)

                @pl.when(
                    jnp.logical_and(
                        since >= 0,
                        jnp.logical_and(
                            since % GRAD_EVERY == 0, since // GRAD_EVERY < own_chunks
                        ),
                    )
                )
                def _():
                    for quarter in quarters:
                        gradient(since // GRAD_EVERY, quarter)

            paced = chunk * per + sub - pace_from

            @pl.when(
                jnp.logical_and(
                    paced >= 0,
                    jnp.logical_and(2 * paced % PACE < 2, 2 * paced // PACE < in_loop),
                )
            )
            def _():
                issue(2 * paced // PACE)

        @pl.when(chunk == 2)
        def _():
            turn_v[...] = tok_v[...].T
            keep_turned.start()

        @pl.when(chunk == GRAD_FIRST - 1)
        def _():
            load_cot.wait()

        return carry

    lax.fori_loop(0, rounds, turn, 0)

    for step in range(steps - DEPTH - THROTTLE, steps - DEPTH):
        onward(step).wait_send()
    for pair in range(steps // 2 - THROTTLE, steps // 2):
        across(pair).wait_send()
    for chunk in range(all_chunks - LENT + 1, all_chunks):
        lend(chunk).wait_send()
    for chunk in range(all_chunks - 3, all_chunks):
        keep_taken(chunk).wait()
    keep_turned.wait()

    def rest(piece, carry):
        issue(piece)
        return carry

    lax.fori_loop(in_loop, pieces, rest, 0)
    for piece in range(pieces - FLYING, pieces):
        sent_piece(piece)

    def drain(piece, carry):
        keep_act(piece).wait()

        @pl.when(piece < own_chunks - LATE)
        def _():
            trade_grad(piece).wait_recv()

        @pl.when(piece >= own_chunks - LATE)
        def _():
            keep_late(piece).wait()

        return carry

    lax.fori_loop(0, own_chunks, drain, 0)


def fused(assignment, lr_index, rates, tokens, weight, momentum, cot, members):
    rows, cols = weight.shape
    count, share = cot.shape
    chunks = cols // CHUNK
    own_chunks = chunks // 2
    per = SPLIT * (CHUNK // SUB)
    chips = members // 2
    fill = (chips - 1) * DEPTH
    steps = 2 * chunks * per + fill + fill % 2
    slots = (fill + LAG + per - 1) // per + 4
    part = rows // 2 // SPLIT
    kind = weight.dtype
    dma = pltpu.SemaphoreType.DMA
    anywhere = pl.BlockSpec(memory_space=pl.ANY)
    return pl.pallas_call(
        functools.partial(fused_kernel, members),
        out_shape=(
            jax.ShapeDtypeStruct((2 * chunks, rows, CHUNK), kind),
            jax.ShapeDtypeStruct((own_chunks - LATE, count, CHUNK), kind),
            jax.ShapeDtypeStruct((own_chunks, count, CHUNK), kind),
            jax.ShapeDtypeStruct((rows, count), kind),
            jax.ShapeDtypeStruct((LATE, count, CHUNK), kind),
        ),
        in_specs=[pl.BlockSpec(memory_space=pltpu.SMEM)] * 3 + [anywhere] * 4,
        out_specs=(anywhere,) * 5,
        scratch_shapes=[
            pltpu.VMEM((steps, part, SUB), kind),
            pltpu.VMEM((steps, part, SUB), kind),
            pltpu.VMEM((slots, rows, CHUNK), kind),
            pltpu.VMEM((LENT, rows // 2, CHUNK), kind),
            pltpu.VMEM((3, rows, CHUNK), kind),
            pltpu.VMEM((own_chunks, count, CHUNK), kind),
            pltpu.VMEM((own_chunks, count, CHUNK), kind),
            pltpu.VMEM((own_chunks, count, CHUNK), kind),
            pltpu.VMEM((2, rows, CHUNK), kind),
            pltpu.VMEM((count, share), kind),
            pltpu.VMEM((count, rows), kind),
            pltpu.VMEM((rows, count), kind),
            dma((slots,)),
            dma((LENT,)),
            dma((2 * chunks,)),
            dma((THROTTLE,)),
            dma((steps,)),
            dma((THROTTLE,)),
            dma((steps // 2,)),
            dma((own_chunks,)),
            dma((own_chunks,)),
            dma((own_chunks,)),
            dma((own_chunks,)),
            dma((3,)),
            dma((own_chunks,)),
            dma((LATE,)),
            dma((2,)),
            dma((3,)),
        ],
        compiler_params=pltpu.CompilerParams(
            collective_id=0, has_side_effects=True, vmem_limit_bytes=60 * 2**20
        ),
        name="fused",
    )(assignment, lr_index, rates, tokens, weight, momentum, cot)


def settle_kernel(first, lr_index, rates, turned, both, grads, extra, out, *rest):
    *active, turn_v, base_v, grad_v, turn_sem, base_sem, grad_sem, out_sem = rest[: len(rest) - 4 * (len(rest) > 8)]
    rows = turned.shape[0]
    chunks = both.shape[0] // 2
    own_chunks = chunks // 2
    count = grad_v.shape[0]
    side = lax.axis_index("tp")
    rate = rates[lr_index[lax.axis_index("pop")]]
    if active:
        copy_v, act_v, copy_sem, act_sem = rest[-4:]

    def each(total, act):
        def body(index, carry):
            act(index)
            return carry

        lax.fori_loop(0, total, body, 0)

    def cut(at):
        return pl.ds(pl.multiple_of(at * CHUNK, CHUNK), CHUNK)

    def far(step):
        return (1 - side) * own_chunks + first + step

    def near(step):
        return side * own_chunks + step

    def load_base(step):
        return pltpu.make_async_copy(
            both.at[chunks + far(step)], base_v.at[step], base_sem.at[step]
        )

    def load_grad(step):
        return pltpu.make_async_copy(grads.at[step], grad_v.at[step], grad_sem.at[step])

    def store(step):
        return pltpu.make_async_copy(base_v.at[step], out.at[:, cut(far(step))], out_sem.at[step])

    def load_copy(step):
        return pltpu.make_async_copy(
            both.at[chunks + near(step)], copy_v.at[step], copy_sem.at[0, step]
        )

    def store_copy(step):
        return pltpu.make_async_copy(
            copy_v.at[step], out.at[:, cut(near(step))], copy_sem.at[1, step]
        )

    def load_act(step):
        return pltpu.make_async_copy(extra.at[step], act_v.at[step], act_sem.at[0, step])

    def store_act(step):
        return pltpu.make_async_copy(
            act_v.at[step], active[0].at[:, cut(step)], act_sem.at[1, step]
        )

    load_turned = pltpu.make_async_copy(turned, turn_v, turn_sem.at[0])
    load_turned.start()

    def begin(step):
        load_base(step).start()
        load_grad(step).start()

    def begin_copy(step):
        load_copy(step).start()
        load_act(step).start()

    each(count, begin)
    if active:
        each(own_chunks, begin_copy)
    load_turned.wait()

    def work(step):
        load_base(step).wait()
        load_grad(step).wait()
        for top in (0, rows // 2):
            at = pl.ds(top, rows // 2)
            grad_weight = jnp.dot(
                turn_v[at, :], grad_v[step], preferred_element_type=jnp.float32
            )
            base = base_v[step, at, :].astype(jnp.float32)
            base_v[step, at, :] = (base - rate * grad_weight).astype(base_v.dtype)
        store(step).start()

    each(count, work)
    if active:

        def hand_on(step):
            load_copy(step).wait()
            store_copy(step).start()
            load_act(step).wait()
            store_act(step).start()

        each(own_chunks, hand_on)
        each(own_chunks, lambda step: store_copy(step).wait())
        each(own_chunks, lambda step: store_act(step).wait())
    each(count, lambda step: store(step).wait())


def settle(first, count, lr_index, rates, turned, both, grads, extra, last):
    rows, tall = turned.shape
    chunks = both.shape[0] // 2
    own_chunks = chunks // 2
    kind = both.dtype
    scalar = pl.BlockSpec(memory_space=pltpu.SMEM)
    anywhere = pl.BlockSpec(memory_space=pl.ANY)
    dma = pltpu.SemaphoreType.DMA
    whole = jax.ShapeDtypeStruct((rows, chunks * CHUNK), kind)
    scratch = [
        pltpu.VMEM((rows, tall), kind),
        pltpu.VMEM((count, rows, CHUNK), kind),
        pltpu.VMEM((count, tall, CHUNK), kind),
        dma((1,)),
        dma((count,)),
        dma((count,)),
        dma((count,)),
    ]
    if not last:
        scratch += [
            pltpu.VMEM((own_chunks, rows, CHUNK), kind),
            pltpu.VMEM((own_chunks, tall, CHUNK), kind),
            dma((2, own_chunks)),
            dma((2, own_chunks)),
        ]
    return pl.pallas_call(
        functools.partial(settle_kernel, first),
        in_specs=[scalar, scalar] + [anywhere] * 4,
        out_specs=anywhere if last else (anywhere, anywhere),
        out_shape=whole
        if last
        else (whole, jax.ShapeDtypeStruct((tall, own_chunks * CHUNK), kind)),
        scratch_shapes=scratch,
        input_output_aliases={5: 0} if last else {},
        compiler_params=pltpu.CompilerParams(
            vmem_limit_bytes=(LATE_LIMIT if last else 60) * 2**20
        ),
        cost_estimate=pl.CostEstimate(
            flops=2 * rows * tall * count * CHUNK,
            bytes_accessed=6 * rows * count * CHUNK,
            transcendentals=0,
        ),
        name="settle_late" if last else "settle",
    )(lr_index, rates, turned, both, grads, extra)


def local(tokens, weight, momentum, cotangent, assignment, lr_index, rates):
    members = lax.axis_size("pop")
    ranks = lax.axis_size("tp")
    me = lax.axis_index("pop")
    side = lax.axis_index("tp")
    if ranks == 2 and assignment.shape[0] // 4 == 1:
        both, grads, act, turned, late_mine = fused(
            assignment.T, lr_index, rates, tokens[0], weight[0], momentum[0], cotangent[0], members
        )
        late_theirs = lax.ppermute(late_mine, "tp", [(0, 1), (1, 0)])
        count = grads.shape[0]
        partly, active = settle(0, count, lr_index, rates, turned, both, grads, act, False)
        late_theirs, partly = lax.optimization_barrier((late_theirs, partly))
        updated = settle(
            count, LATE, lr_index, rates, turned, both, late_theirs, partly, True
        )
        return (active[None], updated[None])
    member_ids = jnp.arange(members, dtype=jnp.int32)
    hit = assignment[:, 0] == me
    my_source = jnp.where(jnp.any(hit), jnp.sum(jnp.where(hit, assignment[:, 1], 0)), me)
    my_index = jnp.sum(jnp.where(member_ids == me, lr_index, 0))
    rate_ids = jnp.arange(rates.shape[0], dtype=jnp.int32)
    my_rate = jnp.sum(jnp.where(rate_ids == my_index, rates, 0.0))
    tops = assignment.shape[0] // 4
    winner_hit = assignment[:, 1][None, :] == member_ids[:, None]
    present = jnp.any(winner_hit, axis=1)
    roots = jnp.sort(jnp.where(present, member_ids, members))[:tops]
    place = ring_of(me, members)
    tables = []
    for turn in range(tops):
        root = roots[turn]
        chips = members // 2
        root_place = ring_of(root, members)
        behind = (place // 2 - root_place // 2 + chips) % chips
        entries = (
            me == root,
            jnp.logical_and(my_source == root, me != root),
            (behind + chips - 1) % chips,
            (2 * chips - behind - 1) % chips,
            jnp.logical_and(place // 2 == root_place // 2, me != root),
        )
        tables.append(jnp.stack([entry.astype(jnp.int32) for entry in entries]))

    def take(value, first, part=0, parts=1):
        taken = None
        for turn in range(tops):
            arrived = spread(value, tables[turn], members, first + turn, part, parts)
            if taken is None:
                taken = arrived
            else:
                taken = jnp.where(my_source == roots[turn], arrived, taken)
        return taken

    inputs = tokens[0]
    share_cols = cotangent.shape[2]
    taken_weight = take(weight[0], 0)
    partial_value = jnp.dot(inputs, taken_weight, preferred_element_type=jnp.float32)
    partial_value = partial_value.astype(jnp.bfloat16)
    if ranks == 2:
        swap = [(0, 1), (1, 0)]
        left, right = partial_value[:, :share_cols], partial_value[:, share_cols:]
        mine = jnp.where(side == 0, left, right)
        theirs = jnp.where(side == 0, right, left)
        theirs, raw_momentum = lax.optimization_barrier((theirs, momentum[0]))
        arrived = lax.ppermute(theirs, "tp", swap)
        first = take(raw_momentum, tops, 0, 2)
        arrived, first = lax.optimization_barrier((arrived, first))
        hidden = mine.astype(jnp.float32) + arrived.astype(jnp.float32)
        active, grad_mine = activate(hidden, cotangent[0])
        grad_mine, raw_momentum = lax.optimization_barrier((grad_mine, raw_momentum))
        grad_theirs = lax.ppermute(grad_mine, "tp", swap)
        second = take(raw_momentum, 2 * tops, 1, 2)
        updated = update(
            side.astype(jnp.int32).reshape(1),
            my_rate.reshape(1),
            inputs.T,
            grad_mine,
            grad_theirs,
            taken_weight,
            first,
            second,
        )
    else:
        taken_momentum = take(momentum[0], tops)
        hidden = lax.psum_scatter(
            partial_value, "tp", scatter_dimension=1, tiled=True
        ).astype(jnp.float32)
        active, grad_mine = activate(hidden, cotangent[0])
        grad_hidden = lax.all_gather(grad_mine, "tp", axis=1, tiled=True)
        grad_weight = lax.dot_general(
            inputs, grad_hidden, (((0,), (0,)), ((), ())), preferred_element_type=jnp.float32
        )
        new_momentum = 0.9 * taken_momentum.astype(jnp.float32) + grad_weight
        updated = taken_weight.astype(jnp.float32) - my_rate * new_momentum
        updated = updated.astype(jnp.bfloat16)
    return (active[None], updated[None])


def solution(mesh):
    placed = (
        P("pop", None, "tp"),
        P("pop", "tp", None),
        P("pop", "tp", None),
        P("pop", None, "tp"),
        P(),
        P(),
        P(),
    )
    return jax.shard_map(
        local,
        mesh=mesh,
        in_specs=placed,
        out_specs=(P("pop", None, "tp"), P("pop", "tp", None)),
        check_vma=False,
    )
```
